32 devices in a mesh: req: 16 (over z, y, x), head: 2 (over core).
Axes of the slice: x: 2, y: 2, z: 4, core: 2. Of those that a mesh axis runs over, the one named last changes fastest.
Arguments:
- queries: bfloat16 [8192, 8192], P('req', 'head'), may hold values from -8 to 8
- keys_values: bfloat16 [8192, 2048], P('req', 'head'), may hold values from -8 to 8
- seg_ids: int32 [8192], replicated, may hold values from -1 to 13, as said below
- cache_page: int32 [512], replicated, may hold values from 0 to 511, as said below
Outputs:
- context: bfloat16 [8192, 8192], P('req', 'head')
- cache: bfloat16 [8192, 2048], P('req', 'head')
The draws below stay inside these ranges and needn't reach their ends.
Inputs may be any that keep to these rules, and one draw needn't show every extreme that they name: `seg_ids`: stream s occupies the 4096 positions that start at s * 4096 + 256, counted modulo 8192: first its shared prompt (id s * 7, at least one token), then its 6 requests in order (ids s * 7 + 1 to s * 7 + 6, each at least one token), then padding: 1 to 255 tokens in every stream but the last, and 256 to 512 tokens in the last, so that positions 0 to 255 are padding. `cache_page`: every cache page is named once. Cache pages d * 32 to d * 32 + 31 belong to index d of req; the 32 token pages of one index of req go to exactly 16 owners, exactly 2 pages to each.
All inputs are finite; a program needn't handle non-finite values.
Results may differ from the reference program's by a relative error of at most 0.0055.
Values may be sent and summed in bfloat16 or wider, within the bound.
A program may use at most 128 MiB of HBM per device.

```python
import jax
import jax.numpy as jnp
from jax import lax

QH = 64
KVH = 8
HD = 128
STREAM = 4096
REQS = 6
PAGE = 16
TOKENS = 8192
NPAGES = 512
PG_DEV = 32
CAP = 2
LEAD = 256
N_REQ = 16


def draw_queries(key, part):
    shape = (TOKENS, KVH, QH // KVH, HD)
    own_key = jax.random.fold_in(key, 1)
    values = jnp.clip(jax.random.normal(own_key, shape, jnp.float32), -6.0, 6.0)
    return values.reshape(TOKENS, QH * HD).astype(jnp.bfloat16)


def draw_keys_values(key, part):
    shape = (TOKENS, KVH, 2, HD)
    own_key = jax.random.fold_in(key, 2)
    values = jnp.clip(jax.random.normal(own_key, shape, jnp.float32), -6.0, 6.0)
    return values.reshape(TOKENS, KVH * 2 * HD).astype(jnp.bfloat16)


def draw_seg_ids(key, part):
    streams = TOKENS // STREAM

    def one_stream(stream_key, stream_index):
        key_pre, key_pad, key_last, key_share = jax.random.split(stream_key, 4)
        prefix = jax.random.randint(key_pre, (), STREAM // 16, STREAM // 4 + 1)
        drawn_pad = jax.random.randint(key_pad, (), 1, STREAM // 16)
        last_pad = jax.random.randint(key_last, (), LEAD, STREAM // 8 + 1)
        padding = jnp.where(stream_index == streams - 1, last_pad, drawn_pad)
        shares = jax.random.randint(key_share, (REQS,), 1, 9)
        running = jnp.cumsum(shares)
        remainder = STREAM - prefix - padding
        bounds = remainder * running[:-1] // running[-1]
        position = jnp.arange(STREAM, dtype=jnp.int32)
        offset = position - prefix
        local_id = 1 + jnp.sum((offset[:, None] >= bounds[None, :]).astype(jnp.int32), axis=1)
        local_id = jnp.where(position < prefix, 0, local_id)
        local_id = jnp.where(position >= prefix + remainder, -1, local_id)
        return jnp.where(local_id >= 0, stream_index * (REQS + 1) + local_id, -1).astype(jnp.int32)
    stream_keys = jax.random.split(key, streams)
    laid = jax.vmap(one_stream)(stream_keys, jnp.arange(streams, dtype=jnp.int32)).reshape(-1)
    return jnp.roll(laid, LEAD, axis=0)


def draw_cache_page(key, part):
    rounds = PG_DEV // CAP
    key_rho, key_sigma, key_offs, key_pis, key_taus = jax.random.split(key, 5)
    owner_perm = jax.random.permutation(key_rho, N_REQ)
    source_perm = jax.random.permutation(key_sigma, N_REQ)
    offsets = jax.random.permutation(key_offs, N_REQ)[:rounds]
    page_perms = jax.vmap(lambda one_key: jax.random.permutation(one_key, PG_DEV))(jax.random.split(key_pis, N_REQ))
    slot_perms = jax.vmap(lambda one_key: jax.random.permutation(one_key, PG_DEV))(jax.random.split(key_taus, N_REQ))
    round_of = page_perms // CAP
    within = page_perms % CAP
    owners = owner_perm[(source_perm[:, None] + offsets[round_of]) % N_REQ]
    slots = slot_perms[owners, round_of * CAP + within]
    return (owners * PG_DEV + slots).reshape(-1).astype(jnp.int32)


def setup_inputs(seed: int = 0) -> dict:
    key_of = jax.random.split(jax.random.key(seed), 5)
    queries = draw_queries(jax.random.fold_in(key_of[4], 71), 0)
    keys_values = draw_keys_values(jax.random.fold_in(key_of[4], 71), 0)
    seg_ids = draw_seg_ids(jax.random.fold_in(key_of[4], 71), 0)
    cache_page = draw_cache_page(jax.random.fold_in(key_of[4], 71), 0)
    return dict(queries=queries, keys_values=keys_values, seg_ids=seg_ids, cache_page=cache_page)


NEG_FILL = -1e+30

def reference(queries, keys_values, seg_ids, cache_page):
    streams = TOKENS // STREAM
    per_group = QH // KVH
    score_scale = 1.0 / jnp.sqrt(jnp.float32(HD))
    rolled_q = jnp.roll(queries, -LEAD, axis=0)
    rolled_kv = jnp.roll(keys_values, -LEAD, axis=0)
    rolled_seg = jnp.roll(seg_ids, -LEAD, axis=0)
    query_split = rolled_q.reshape(streams, STREAM, KVH, per_group, HD)
    pair_split = rolled_kv.reshape(streams, STREAM, KVH, 2, HD)
    seg_split = rolled_seg.reshape(streams, STREAM)
    position = jnp.arange(STREAM, dtype=jnp.int32)

    def per_stream(item):
        stream_q, stream_kv, stream_seg = item
        shared = stream_seg // (REQS + 1) * (REQS + 1)
        is_live = stream_seg >= 0
        visible = is_live[:, None] & (stream_seg[None, :] >= 0) & (position[None, :] <= position[:, None])
        visible = visible & ((stream_seg[None, :] == stream_seg[:, None]) | (stream_seg[None, :] == shared[:, None]))

        def per_head(head_item):
            head_q, head_k, head_v = head_item
            scores = jnp.einsum('qrd,kd->rqk', head_q.astype(jnp.float32), head_k.astype(jnp.float32)) * score_scale
            scores = jnp.where(visible[None], scores, NEG_FILL)
            row_top = lax.optimization_barrier(jnp.max(scores, axis=-1))
            weight = jnp.where(visible[None], jnp.exp(scores - row_top[..., None]), 0.0)
            row_total = lax.optimization_barrier(jnp.sum(weight, axis=-1))
            weight_low = lax.optimization_barrier(weight.astype(jnp.bfloat16)).astype(jnp.float32)
            weighted = jnp.einsum('rqk,kd->rqd', weight_low, head_v.astype(jnp.float32))
            safe_total = jnp.where(is_live[None, :], row_total, 1.0)
            return jnp.where(is_live[None, :, None], weighted / safe_total[..., None], 0.0)
        heads_out = lax.map(per_head, (jnp.transpose(stream_q, (1, 0, 2, 3)), jnp.transpose(stream_kv[:, :, 0, :], (1, 0, 2)), jnp.transpose(stream_kv[:, :, 1, :], (1, 0, 2))))
        return jnp.transpose(heads_out, (2, 0, 1, 3)).reshape(STREAM, QH * HD)
    context = lax.map(per_stream, (query_split, pair_split, seg_split)).reshape(TOKENS, QH * HD).astype(jnp.bfloat16)
    context = jnp.roll(context, LEAD, axis=0)
    live_rows = (seg_ids >= 0)[:, None]
    masked = jnp.where(live_rows, keys_values, jnp.zeros_like(keys_values)).reshape(NPAGES, PAGE, KVH * 2 * HD)
    cache = jnp.zeros_like(masked).at[cache_page].set(masked).reshape(TOKENS, KVH * 2 * HD)
    return (context, cache)
```

```python
import functools
import math

import jax
import jax.numpy as jnp
from jax import lax
from jax.experimental import pallas as pl
from jax.experimental.pallas import tpu as pltpu
from jax.sharding import PartitionSpec as P

HD = 128
STREAM = 4096
REQS = 6
PAGE = 16

NEG_FILL = -1e30
TILE_Q = 128
TILE_K = 256
CHUNK_HEADS = 4
CHUNK = 256
LEAD = 256
PROMPT_CHUNKS = 4
NEAR = 2
FACTOR = math.log2(math.e) / math.sqrt(HD)
MESH = pl.DeviceIdType.MESH

ROUNDS = (
    ((0, 1, 0), (0, 2, 0), (0, 4, 0), (1, 0, 2), (1, 3, 1), (1, 5, 1), (2, 3, 3), (2, 6, 4), (3, 1, 5), (3, 7, 6), (4, 5, 7), (4, 6, 7), (5, 7, 9), (6, 7, 11), (6, 10, 12), (7, 5, 13), (7, 11, 14)),
    ((0, 2, 2), (0, 4, 2), (1, 3, 2), (1, 5, 5), (2, 3, 4), (2, 6, 3), (3, 2, 1), (3, 7, 3), (4, 5, 8), (4, 6, 0), (4, 8, 0), (5, 4, 1), (5, 7, 10), (5, 9, 13), (6, 4, 4), (6, 7, 12), (6, 10, 11), (7, 5, 6), (7, 6, 9), (10, 8, 12), (11, 9, 14)),
    ((1, 5, 0), (2, 3, 0), (2, 6, 2), (3, 7, 2), (4, 5, 2), (4, 6, 8), (4, 8, 1), (5, 4, 5), (5, 7, 1), (6, 4, 3), (6, 7, 0), (6, 10, 3), (7, 5, 3), (7, 6, 10), (9, 8, 14), (10, 8, 11)),
    ((4, 8, 2), (5, 4, 6), (7, 6, 1), (9, 8, 13), (10, 8, 3)),
)


def plan_of(rounds, count, group):
    held = [{2 * i - 1: 0, 2 * i: 1} for i in range(count)]
    sends = [[[] for _ in range(count)] for _ in rounds]
    takes = [[[] for _ in range(count)] for _ in rounds]
    for index, transfers in enumerate(rounds):
        fresh = []
        for base in range(0, count, group):
            for source, target, chunk in transfers:
                u, v, c = base + source, base + target, 2 * base + chunk
                if u >= count or v >= count:
                    continue
                slot = len(held[v]) + sum(1 for w, _, _ in fresh if w == v)
                fresh.append((v, c, slot))
                sends[index][u].append((v, held[u][c], slot, len(takes[index][v])))
                takes[index][v].append(slot)
        for v, c, slot in fresh:
            held[v][c] = slot
    slots = max(len(h) for h in held)
    lows = [[None] * slots for _ in range(count)]
    for i, chunks in enumerate(held):
        for c, slot in chunks.items():
            lows[i][slot] = LEAD + c * CHUNK
    return sends, takes, slots, lows


def at_device(values, me):
    common = max(set(values), key=values.count)
    result = common
    for i, value in enumerate(values):
        if value != common:
            result = jnp.where(me == i, value, result)
    return result


def place_rows(out_ref, from_ref, source_ref, live_ref):
    height = source_ref.shape[0]
    at = lax.broadcasted_iota(jnp.int32, (PLACE_ROWS, height), 1)
    for first in range(0, out_ref.shape[0], PLACE_ROWS):
        rows = pl.ds(first, PLACE_ROWS)
        chosen = from_ref[rows, 0:1] == at
        if live_ref is not None:
            chosen = chosen & (live_ref[0:1, :] > 0)
        one_hot = jnp.where(chosen, 1.0, 0.0).astype(source_ref.dtype)
        out_ref[rows, :] = jnp.dot(
            one_hot, source_ref[...], preferred_element_type=jnp.float32
        ).astype(out_ref.dtype)


def exchange_kernel(plan, count, heads, capacity, page_ref, arrival_ref, live_ref, kv_ref, win_ref, cache_ref, stage,
                    incoming, own_sem, send_sem, recv_sem, page_send, page_recv, self_sem):
    sends, takes, slots, _ = plan
    me = lax.axis_index("req")
    rounds = len(sends)
    wide = kv_ref.shape[1] // heads
    block = capacity * PAGE
    own = pltpu.make_async_copy(kv_ref, win_ref.at[0 : 2 * CHUNK, :], own_sem)
    own.start()
    barrier = pltpu.get_barrier_semaphore()

    def greet(offset, carry):
        pl.semaphore_signal(
            barrier, inc=1, device_id={"req": lax.rem(me + offset, count)}, device_id_type=MESH
        )
        return carry

    lax.fori_loop(1, count, greet, 0)

    place_rows(stage, page_ref, kv_ref, live_ref)
    pl.semaphore_wait(barrier, count - 1)

    def copy_of(r, k, g, target, from_own, src_row, dst_row):
        columns = pl.ds(g * wide, wide)
        source = (kv_ref if from_own else win_ref).at[pl.ds(src_row, CHUNK), columns]
        return pltpu.make_async_remote_copy(
            src_ref=source,
            dst_ref=win_ref.at[pl.ds(dst_row, CHUNK), columns],
            send_sem=send_sem.at[r, k[0], g],
            recv_sem=recv_sem.at[r, k[1], g],
            device_id={"req": target},
            device_id_type=MESH,
        )

    outgoing = []
    for r in range(rounds):
        row = []
        for j in range(max(len(s) for s in sends[r])):
            live = [i for i in range(count) if len(sends[r][i]) > j]
            get = lambda f: at_device([f(sends[r][i][j]) if i in live else -1 for i in range(count)], me)
            target, slot, dst, k = (get(lambda s, c=c: s[c]) for c in range(4))
            row.append((j, target, slot, dst, k))
        outgoing.append(row)
    takes_here = [
        [
            at_device([takes[r][i][k] if len(takes[r][i]) > k else -1 for i in range(count)], me)
            for k in range(max(len(t) for t in takes[r]))
        ]
        for r in range(rounds)
    ]

    def arrive(r, g):
        for k, slot in enumerate(takes_here[r]):
            @pl.when(slot >= 0)
            def _():
                dst = pl.multiple_of(slot * CHUNK, CHUNK)
                copy_of(r, (0, k), g, me, False, dst, dst).wait_recv()

    def launch(r, g):
        for j, target, slot, dst, k in outgoing[r]:
            place = pl.multiple_of(dst * CHUNK, CHUNK)
            from_row = pl.multiple_of(slot * CHUNK, CHUNK)

            @pl.when((target >= 0) & (slot < 2))
            def _():
                copy_of(r, (j, k), g, target, True, from_row, place).start()

            if r > 0:
                @pl.when((target >= 0) & (slot >= 2))
                def _():
                    copy_of(r, (j, k), g, target, False, from_row, place).start()

    def page_copy(offset):
        target = lax.rem(me + offset, count)
        return pltpu.make_async_remote_copy(
            src_ref=stage.at[pl.ds(pl.multiple_of(target * block, block), block), :],
            dst_ref=incoming.at[pl.ds(pl.multiple_of(offset * block, block), block), :],
            send_sem=page_send.at[offset],
            recv_sem=page_recv.at[offset],
            device_id={"req": target},
            device_id_type=MESH,
        )

    def send_pages(offset, carry):
        page_copy(offset).start()
        return carry

    for tick in range(rounds + heads - 1):
        for r in range(rounds - 1, -1, -1):
            g = tick - r
            if 0 <= g < heads:
                if r > 0:
                    arrive(r - 1, g)
                launch(r, g)
        if tick == PAGES_AT:
            lax.fori_loop(1, count, send_pages, 0)
    mine = pltpu.make_async_copy(
        stage.at[pl.ds(pl.multiple_of(me * block, block), block), :], incoming.at[0:block, :], self_sem
    )
    mine.start()
    for g in range(heads):
        arrive(rounds - 1, g)
    for r in range(rounds):
        for g in range(heads):
            for j, target, slot, dst, k in outgoing[r]:
                @pl.when(target >= 0)
                def _():
                    copy_of(r, (j, 0), g, me, True, 0, 0).wait_send()

    def take_pages(offset, carry):
        page_copy(offset).wait()
        return carry

    lax.fori_loop(1, count, take_pages, 0)
    mine.wait()
    own.wait()

    place_rows(cache_ref, arrival_ref, incoming, None)


PAGES_AT = 1
PLACE_ROWS = 128


def exchange(plan, keys_values, live, send_page, arrival, heads, capacity, collective_id):
    sends, takes, slots, _ = plan
    count = lax.axis_size("req")
    rows, cols = keys_values.shape
    rounds = len(sends)
    outs = max(len(s) for r in sends for s in r)
    ins = max(len(t) for r in takes for t in r)
    vmem = pl.BlockSpec(memory_space=pltpu.VMEM)
    dma = pltpu.SemaphoreType.DMA
    return pl.pallas_call(
        functools.partial(exchange_kernel, plan, count, heads, capacity),
        out_shape=[
            jax.ShapeDtypeStruct((slots * CHUNK, cols), keys_values.dtype),
            jax.ShapeDtypeStruct((rows, cols), keys_values.dtype),
        ],
        in_specs=[vmem] * 4,
        out_specs=[vmem, vmem],
        scratch_shapes=[
            pltpu.VMEM((count * capacity * PAGE, cols), keys_values.dtype),
            pltpu.VMEM((count * capacity * PAGE, cols), keys_values.dtype),
            dma,
            dma((rounds, outs, heads)),
            dma((rounds, ins, heads)),
            dma((count,)),
            dma((count,)),
            dma,
        ],
        compiler_params=pltpu.CompilerParams(
            collective_id=collective_id, has_side_effects=True, vmem_limit_bytes=48 << 20
        ),
        name="exchange",
    )(send_page, arrival, live, keys_values)


def answer_kernel(per_group, slots, counts, table, lows, info_ref, q_ref, kv_ref, out_ref, bias, keys, values):
    g, t = pl.program_id(0), pl.program_id(1)
    tile_q = q_ref.shape[0]
    begin, stop, own, row = (info_ref[:, c : c + 1] for c in range(4))
    pair = 2 if per_group % 2 == 0 else 1
    parts = per_group // pair

    @pl.when((g == 0) & (t == 0))
    def _():
        values[:, HD:] = jnp.ones((values.shape[0], HD), values.dtype)

    def tile(blocks):
        span = blocks * TILE_K
        for s in range(blocks):
            start = pl.multiple_of(table[t, s] * TILE_K, TILE_K)
            keys[s * TILE_K : (s + 1) * TILE_K, :] = kv_ref[pl.ds(start, TILE_K), 0:HD]
            values[s * TILE_K : (s + 1) * TILE_K, 0:HD] = kv_ref[pl.ds(start, TILE_K), HD : 2 * HD]

        @pl.when(g == 0)
        def _():
            for s in range(blocks):
                at = lows[table[t, s]] + lax.broadcasted_iota(jnp.int32, (tile_q, TILE_K), 1)
                seen = (at <= row) & ((at >= own) | ((at >= begin) & (at < stop)))
                bias[t, :, s * TILE_K : (s + 1) * TILE_K] = jnp.where(seen, 0.0, NEG_FILL).astype(jnp.float32)

        def score(part):
            stacked = jnp.concatenate(
                [q_ref[:, h * HD : (h + 1) * HD] for h in range(part * pair, (part + 1) * pair)], axis=0
            )
            raw = lax.dot_general(
                stacked, keys[0:span, :], (((1,), (1,)), ((), ())), preferred_element_type=jnp.float32
            )
            return (raw.reshape(pair, tile_q, span) + bias[t, :, 0:span][None]).reshape(pair * tile_q, span)

        live = jnp.concatenate([row >= own] * pair, axis=0)
        ahead = score(0)
        for part in range(parts):
            now = ahead
            if part + 1 < parts:
                ahead = score(part + 1)
            top = jnp.max(now, axis=1, keepdims=True)
            weight = jnp.exp2((now - top) * FACTOR).astype(values.dtype)
            both = jnp.dot(weight, values[0:span, :], preferred_element_type=jnp.float32)
            total = jnp.where(live, both[:, HD:], 1.0)
            context = jnp.where(live, both[:, 0:HD] / total, 0.0).astype(out_ref.dtype)
            for i in range(pair):
                h = part * pair + i
                out_ref[:, h * HD : (h + 1) * HD] = context[i * tile_q : (i + 1) * tile_q, :]

    @pl.when(counts[t] == 0)
    def _():
        out_ref[...] = jnp.zeros_like(out_ref)

    for blocks in range(1, slots + 1):
        @pl.when(counts[t] == blocks)
        def _():
            tile(blocks)


def block_table(lows, info, tiles, tile_q):
    blocks = lows.shape[0]
    low = lows[None, :]
    high = low + TILE_K
    begin, stop, own, row = (info[:, c : c + 1] for c in range(4))
    end = jnp.minimum(stop, row + 1)
    touched = ((low < end) & (high > begin)) | ((low <= row) & (high > own))
    whole = ((low >= begin) & (high <= end)) | ((low >= own) & (high <= row + 1))
    touched = jnp.any(touched.reshape(tiles, tile_q, blocks), axis=1)
    whole = jnp.all(whole.reshape(tiles, tile_q, blocks), axis=1)
    kind = jnp.where(touched, jnp.where(whole, 2, 1), 0).astype(jnp.int32)
    counts = jnp.sum(touched.astype(jnp.int32), axis=1)
    slots = jnp.arange(blocks, dtype=jnp.int32)
    before = touched[:, None, :] & (slots[None, None, :] < slots[None, :, None])
    place = jnp.sum(before.astype(jnp.int32), axis=2)
    pick = touched[:, None, :] & (place[:, None, :] == slots[None, :, None])
    table = jnp.sum(jnp.where(pick, slots[None, None, :], 0), axis=2)
    kinds = jnp.sum(jnp.where(pick, kind[:, None, :], 0), axis=2)
    return counts, table, kinds


def answer_window(queries, window, lows, info, key_heads, per_group):
    shard_rows = queries.shape[0]
    tile_q = TILE_Q
    tiles = shard_rows // tile_q
    slots = lows.shape[0]
    counts, table, _ = block_table(lows, info, tiles, tile_q)
    wide = per_group * HD
    flops = 4 * shard_rows * key_heads * wide * 1536
    return pl.pallas_call(
        functools.partial(answer_kernel, per_group, slots),
        out_shape=jax.ShapeDtypeStruct(queries.shape, jnp.bfloat16),
        grid_spec=pltpu.PrefetchScalarGridSpec(
            num_scalar_prefetch=3,
            grid=(key_heads, tiles),
            in_specs=[
                pl.BlockSpec((tile_q, info.shape[1]), lambda g, t, *_: (t, 0)),
                pl.BlockSpec((tile_q, wide), lambda g, t, *_: (t, g)),
                pl.BlockSpec((slots * CHUNK, 2 * HD), lambda g, t, *_: (0, g)),
            ],
            out_specs=pl.BlockSpec((tile_q, wide), lambda g, t, *_: (t, g)),
            scratch_shapes=[
                pltpu.VMEM((tiles, tile_q, slots * TILE_K), jnp.float32),
                pltpu.VMEM((slots * TILE_K, HD), jnp.bfloat16),
                pltpu.VMEM((slots * TILE_K, 2 * HD), jnp.bfloat16),
            ],
        ),
        compiler_params=pltpu.CompilerParams(vmem_limit_bytes=48 << 20),
        cost_estimate=pl.CostEstimate(
            flops=flops, bytes_accessed=4 * queries.size + 2 * window.size, transcendentals=flops // (4 * HD)
        ),
        name="answer",
    )(counts, table, lows, info, queries, window)


def from_before(keys_values, group, offset):
    count = lax.axis_size("req")
    pairs = [
        (base + a, base + a + offset)
        for base in range(0, count, group)
        for a in range(group)
        if a + offset <= group and base + a + offset < count
    ]
    return lax.ppermute(keys_values, "req", pairs) if pairs else jnp.zeros_like(keys_values)


def full_window(keys_values, group, own_index):
    shard_rows = keys_values.shape[0]
    pieces = [from_before(keys_values, group, offset) for offset in range(group, 0, -1)]
    blocks = (group + 1) * shard_rows // TILE_K
    first = (own_index - group) * shard_rows
    return pieces + [keys_values], first + jnp.arange(blocks, dtype=jnp.int32) * TILE_K


def attend_kernel(
    pieces, tile_k, per_group, counts, blocks, kinds, lows, info_ref, q_ref, *refs
):
    kv_refs = refs[:pieces]
    refs = refs[pieces:]
    out_ref, kv, stacked, top, acc = refs
    tile = pl.program_id(1)
    tile_q = q_ref.shape[0]

    @pl.when(tile == 0)
    def _():
        at = 0
        for ref in kv_refs:
            kv[at : at + ref.shape[0], :] = ref[...]
            at += ref.shape[0]

    for head in range(per_group):
        stacked[pl.ds(head * tile_q, tile_q), :] = q_ref[:, head * HD : (head + 1) * HD]
    top[...] = jnp.full_like(top, NEG_FILL)
    acc[...] = jnp.zeros_like(acc)
    begin = info_ref[:, 0:1]
    stop = info_ref[:, 1:2]
    own = info_ref[:, 2:3]
    row = info_ref[:, 3:4]
    ones = jnp.ones((tile_k, HD), jnp.bfloat16)

    def block(slot, masked):
        start = pl.multiple_of(blocks[tile, slot] * tile_k, tile_k)
        key = kv[pl.ds(start, tile_k), 0:HD]
        value = jnp.concatenate([kv[pl.ds(start, tile_k), HD : 2 * HD], ones], axis=1)
        if masked:
            at = lows[blocks[tile, slot]] + lax.broadcasted_iota(jnp.int32, (tile_q, tile_k), 1)
            seen = (at <= row) & ((at >= own) | ((at >= begin) & (at < stop)))
            bias = jnp.where(seen, 0.0, NEG_FILL).astype(jnp.float32)
        chunk = min(CHUNK_HEADS, per_group)
        rows = chunk * tile_q
        for part in range(per_group // chunk):
            span = pl.ds(part * rows, rows)
            score = lax.dot_general(
                stacked[span, :], key, (((1,), (1,)), ((), ())),
                preferred_element_type=jnp.float32,
            )
            if masked:
                score = (score.reshape(chunk, tile_q, tile_k) + bias[None]).reshape(rows, tile_k)
            old = top[span, :]
            new = jnp.maximum(old, jnp.max(score, axis=1, keepdims=True))
            rescale = jnp.exp2((old - new) * FACTOR)
            weight = jnp.exp2((score - jnp.tile(new, (1, tile_k // HD))) * FACTOR)
            acc[span, :] = acc[span, :] * jnp.tile(rescale, (1, 2)) + jnp.dot(
                weight.astype(jnp.bfloat16), value, preferred_element_type=jnp.float32
            )
            top[span, :] = new

    def step(slot, carry):
        @pl.when(kinds[tile, slot] == 1)
        def _():
            block(slot, True)

        @pl.when(kinds[tile, slot] == 2)
        def _():
            block(slot, False)

        return carry

    lax.fori_loop(0, counts[tile], step, 0)
    live = row >= own
    for head in range(per_group):
        span = pl.ds(head * tile_q, tile_q)
        total = jnp.where(live, acc[span, HD : 2 * HD], 1.0)
        context = jnp.where(live, acc[span, 0:HD] / total, 0.0)
        out_ref[:, head * HD : (head + 1) * HD] = context.astype(out_ref.dtype)


def attend(queries, pieces, lows, info, key_heads, per_group):
    shard_rows = queries.shape[0]
    tile_q = min(TILE_Q, shard_rows)
    tile_k = TILE_K
    span_rows = sum(piece.shape[0] for piece in pieces)
    tiles = shard_rows // tile_q
    counts, table, kinds = block_table(lows, info, tiles, tile_q)
    wide = per_group * HD
    rows = per_group * tile_q
    flops = 4 * shard_rows * key_heads * wide * 1536
    return pl.pallas_call(
        functools.partial(attend_kernel, len(pieces), tile_k, per_group),
        out_shape=jax.ShapeDtypeStruct(queries.shape, jnp.bfloat16),
        grid_spec=pltpu.PrefetchScalarGridSpec(
            num_scalar_prefetch=4,
            grid=(key_heads, tiles),
            in_specs=[
                pl.BlockSpec((tile_q, info.shape[1]), lambda g, t, *_: (t, 0)),
                pl.BlockSpec((tile_q, wide), lambda g, t, *_: (t, g)),
            ]
            + [pl.BlockSpec((p.shape[0], 2 * HD), lambda g, t, *_: (0, g)) for p in pieces],
            out_specs=pl.BlockSpec((tile_q, wide), lambda g, t, *_: (t, g)),
            scratch_shapes=[
                pltpu.VMEM((span_rows, 2 * HD), jnp.bfloat16),
                pltpu.VMEM((rows, HD), jnp.bfloat16),
                pltpu.VMEM((rows, HD), jnp.float32),
                pltpu.VMEM((rows, 2 * HD), jnp.float32),
            ],
        ),
        compiler_params=pltpu.CompilerParams(vmem_limit_bytes=48 << 20),
        cost_estimate=pl.CostEstimate(
            flops=flops, bytes_accessed=4 * queries.size + 2 * span_rows * key_heads * 2 * HD,
            transcendentals=flops // (4 * HD),
        ),
        name="attend",
    )(counts, table, kinds, lows, info, queries, *pieces)


def pick_kernel(pages, index, source_ref, out_ref):
    def move(slot, carry):
        source = pl.multiple_of(index[slot] * PAGE, PAGE)
        target = pl.multiple_of(slot * PAGE, PAGE)
        out_ref[pl.ds(target, PAGE), :] = source_ref[pl.ds(source, PAGE), :]
        return carry

    lax.fori_loop(0, pages, move, 0)


def pick_pages(source, index):
    pages = index.shape[0]
    width = source.shape[1]
    return pl.pallas_call(
        functools.partial(pick_kernel, pages),
        out_shape=jax.ShapeDtypeStruct((pages * PAGE, width), source.dtype),
        grid_spec=pltpu.PrefetchScalarGridSpec(
            num_scalar_prefetch=1,
            grid=(1,),
            in_specs=[pl.BlockSpec(source.shape, lambda i, *_: (0, 0))],
            out_specs=pl.BlockSpec((pages * PAGE, width), lambda i, *_: (0, 0)),
        ),
        cost_estimate=pl.CostEstimate(
            flops=0, bytes_accessed=2 * (source.size + pages * PAGE * width), transcendentals=0
        ),
        name="pick",
    )(index, source)


def page_routes(cache_page, page_count, own_index, axis_size):
    capacity = (page_count + axis_size - 1) // axis_size
    all_pages = cache_page.shape[0]
    owners = cache_page // page_count
    by_source = owners.reshape(axis_size, page_count)
    page_iota = jnp.arange(page_count, dtype=jnp.int32)
    earlier = page_iota[None, :] < page_iota[:, None]
    same_owner = by_source[:, :, None] == by_source[:, None, :]
    rank = jnp.sum((same_owner & earlier[None]).astype(jnp.int32), axis=2)
    my_owner = lax.dynamic_index_in_dim(by_source, own_index, 0, keepdims=False)
    my_rank = lax.dynamic_index_in_dim(rank, own_index, 0, keepdims=False)
    target_slot = my_owner * capacity + my_rank
    slot_iota = jnp.arange(axis_size * capacity, dtype=jnp.int32)
    send_page = jnp.sum(
        jnp.where(slot_iota[:, None] == target_slot[None, :], page_iota[None, :], 0), axis=1
    )
    wanted = own_index * page_count + page_iota
    hits = cache_page[None, :] == wanted[:, None]
    source = jnp.arange(all_pages, dtype=jnp.int32) // page_count
    ranks = rank.reshape(-1)

    def arrival(place):
        return jnp.sum(jnp.where(hits, (place(source) * capacity + ranks)[None, :], 0), axis=1)

    return send_page, arrival, capacity


def rows_of(pages):
    rows = pages[:, None] * PAGE + jnp.arange(PAGE, dtype=jnp.int32)[None, :]
    return jnp.tile(rows.reshape(-1, 1), (1, 8))


def write_pages(keys_values, is_live, cache_page, own_index, axis_size, pieces):
    page_count = keys_values.shape[0] // PAGE
    send_page, arrival, _ = page_routes(cache_page, page_count, own_index, axis_size)
    masked = jnp.where(is_live[:, None], keys_values, jnp.zeros_like(keys_values))
    outgoing = pick_pages(masked, send_page)
    outgoing, pieces = lax.optimization_barrier((outgoing, pieces))
    incoming = lax.all_to_all(outgoing, "req", split_axis=0, concat_axis=0, tiled=True)
    return pick_pages(incoming, arrival(lambda source: source)), pieces


def on_device(queries, keys_values, seg_ids, cache_page):
    shard_rows = queries.shape[0]
    key_heads = keys_values.shape[1] // (2 * HD)
    per_group = queries.shape[1] // HD // key_heads
    tokens = seg_ids.shape[0]
    own_index = lax.axis_index("req")
    axis_size = lax.axis_size("req")
    group = STREAM // shard_rows

    ids = jnp.arange(tokens // STREAM * (REQS + 1), dtype=jnp.int32)
    position = jnp.arange(tokens, dtype=jnp.int32)
    member = seg_ids[None, :] == ids[:, None]
    starts = jnp.min(jnp.where(member, position[None, :], tokens), axis=1)
    stops = jnp.max(jnp.where(member, position[None, :], -1), axis=1) + 1

    query_rows = own_index * shard_rows + jnp.arange(shard_rows, dtype=jnp.int32)
    query_seg = lax.dynamic_slice_in_dim(seg_ids, own_index * shard_rows, shard_rows)
    is_live = query_seg >= 0
    shared = query_seg // (REQS + 1) * (REQS + 1)
    far = 2 * tokens
    is_shared = shared[:, None] == ids[None, :]
    is_own = query_seg[:, None] == ids[None, :]
    begin = jnp.sum(jnp.where(is_shared, starts[None, :], 0), axis=1)
    stop = jnp.sum(jnp.where(is_shared, stops[None, :], 0), axis=1)
    own = jnp.sum(jnp.where(is_own, starts[None, :], 0), axis=1)
    begin = jnp.where(is_live, begin, far)
    stop = jnp.where(is_live, stop, 0)
    own = jnp.where(is_live, own, far)
    zero = jnp.zeros_like(own)
    info = jnp.stack([begin, stop, own, query_rows, zero, zero, zero, zero], axis=1)

    def whole_stream(q, kv):
        pieces, lows = full_window(kv, group, own_index)
        cache, pieces = write_pages(kv, is_live, cache_page, own_index, axis_size, pieces)
        return attend(q, pieces, lows, info, key_heads, per_group), cache

    def windowed(rounds, collective_id, q, kv):
        plan = plan_of(rounds, axis_size, group)
        table = jnp.asarray([[2 * tokens if low is None else low for low in row] for row in plan[3]], jnp.int32)
        lows = lax.dynamic_index_in_dim(table, own_index, 0, keepdims=False)
        send_page, arrival, capacity = page_routes(cache_page, shard_rows // PAGE, own_index, axis_size)
        arrived = arrival(lambda source: (own_index - source + axis_size) % axis_size)
        live = jnp.tile(is_live.astype(jnp.int32)[None, :], (8, 1))
        window, cache = exchange(
            plan, kv, live, rows_of(send_page), rows_of(arrived), key_heads, capacity, collective_id
        )
        return answer_window(q, window, lows, info, key_heads, per_group), cache

    prompt_ok = stops <= ids // (REQS + 1) * STREAM + LEAD + PROMPT_CHUNKS * CHUNK
    request_ok = (stops - 1) // shard_rows - starts // shard_rows <= NEAR
    short = jnp.all(jnp.where(ids % (REQS + 1) == 0, prompt_ok, request_ok))
    if group == 8 and shard_rows == 2 * CHUNK:
        context, cache = lax.cond(
            short, functools.partial(windowed, ROUNDS, 0), whole_stream, queries, keys_values
        )
    else:
        context, cache = whole_stream(queries, keys_values)
    return (context, cache)


def solution(mesh):
    return jax.shard_map(
        on_device,
        mesh=mesh,
        in_specs=(P("req", "head"), P("req", "head"), P(), P()),
        out_specs=(P("req", "head"), P("req", "head")),
        check_vma=False,
    )
```

```python
import functools
import math

import jax
import jax.numpy as jnp
from jax import lax
from jax.experimental import pallas as pl
from jax.experimental.pallas import tpu as pltpu
from jax.sharding import PartitionSpec as P

HD = 128
STREAM = 4096
REQS = 6
PAGE = 16

NEG_FILL = -1e30
TILE_Q = 128
TILE_K = 256
CHUNK_HEADS = 4
CHUNK = 256
LEAD = 256
PROMPT_CHUNKS = 4
NEAR = 2
FACTOR = math.log2(math.e) / math.sqrt(HD)
MESH = pl.DeviceIdType.MESH

ROUNDS = (
    ((0, 1, 0), (0, 2, 0), (0, 4, 0), (1, 0, 2), (1, 3, 1), (1, 5, 1), (2, 3, 3), (2, 6, 4), (3, 1, 5), (3, 7, 6), (4, 5, 7), (4, 6, 7), (5, 7, 9), (6, 7, 11), (6, 10, 12), (7, 5, 13), (7, 11, 14)),
    ((0, 2, 2), (0, 4, 2), (1, 3, 2), (1, 5, 5), (2, 3, 4), (2, 6, 3), (3, 2, 1), (3, 7, 3), (4, 5, 8), (4, 6, 0), (4, 8, 0), (5, 4, 1), (5, 7, 10), (5, 9, 13), (6, 4, 4), (6, 7, 12), (6, 10, 11), (7, 5, 6), (7, 6, 9), (10, 8, 12), (11, 9, 14)),
    ((1, 5, 0), (2, 3, 0), (2, 6, 2), (3, 7, 2), (4, 5, 2), (4, 6, 8), (4, 8, 1), (5, 4, 5), (5, 7, 1), (6, 4, 3), (6, 7, 0), (6, 10, 3), (7, 5, 3), (7, 6, 10), (9, 8, 14), (10, 8, 11)),
    ((4, 8, 2), (5, 4, 6), (7, 6, 1), (9, 8, 13), (10, 8, 3)),
)


def plan_of(rounds, count, group, near):
    places = PROMPT_CHUNKS + near
    own = {i: {2 * i - 1: places, 2 * i: places + 1} for i in range(count)}
    held = [dict(own[i]) for i in range(count)]
    used = [[0, 0] for _ in range(count)]
    sends = [[[] for _ in range(count)] for _ in rounds]
    takes = [[[] for _ in range(count)] for _ in rounds]
    for index, transfers in enumerate(rounds):
        fresh = []
        for base in range(0, count, group):
            for source, target, chunk in transfers:
                u, v, c = base + source, base + target, 2 * base + chunk
                if u >= count or v >= count:
                    continue
                first = 2 * target - 1
                seen = target <= group and chunk < first and (chunk < PROMPT_CHUNKS or chunk >= first - near)
                slot = used[v][0] if seen else places + 2 + used[v][1]
                used[v][0 if seen else 1] += 1
                fresh.append((v, c, slot))
                sends[index][u].append((v, held[u][c], slot, len(takes[index][v])))
                takes[index][v].append(slot)
        for v, c, slot in fresh:
            held[v][c] = slot
    slots = 1 + max(slot for h in held for slot in h.values())
    lows = [[None] * (places + 2) for _ in range(count)]
    for i, chunks in enumerate(held):
        for c, slot in chunks.items():
            if slot < places + 2:
                lows[i][slot] = LEAD + c * CHUNK
    return sends, takes, slots, lows


def at_device(values, me):
    common = max(set(values), key=values.count)
    result = common
    for i, value in enumerate(values):
        if value != common:
            result = jnp.where(me == i, value, result)
    return result


def column_of(ref, row, first, count):
    lanes = ref[row : row + 1, first : first + count]
    return jnp.transpose(jnp.broadcast_to(lanes, (8, count)))[:, 0:1]


def place_rows(out_ref, from_ref, from_row, source_ref, live_ref, live_row):
    height = source_ref.shape[0]
    at = lax.broadcasted_iota(jnp.int32, (PLACE_ROWS, height), 1)
    for first in range(0, out_ref.shape[0], PLACE_ROWS):
        chosen = column_of(from_ref, from_row, first, PLACE_ROWS) == at
        if live_ref is not None:
            chosen = chosen & (live_ref[live_row : live_row + 1, :] > 0)
        one_hot = jnp.where(chosen, 1.0, 0.0).astype(source_ref.dtype)
        out_ref[first : first + PLACE_ROWS, :] = jnp.dot(
            one_hot, source_ref[...], preferred_element_type=jnp.float32
        ).astype(out_ref.dtype)


def stream_kernel(plan, count, heads, per_group, capacity, page_ref, facts_ref, q_hbm, kv_hbm,
                  out_hbm, cache_ref, win, q, stage, incoming, values, bias, done, info_ref, own_sem, q_sem, send_sem, recv_sem,
                  page_send, page_recv, self_sem, out_sem):
    sends, takes, _, lows = plan
    me = lax.axis_index("req")
    rounds = len(sends)
    places = len(lows[0]) - 2
    own_rows = pl.ds(places * CHUNK, 2 * CHUNK)
    wide = 2 * HD
    span_q = per_group * HD
    tiles = q.shape[0] // TILE_Q
    steps = heads * tiles
    pages_at = max(0, min(steps - 1, STAGGER * (heads - 1) - 1))
    block = capacity * PAGE
    fetch_kv = pltpu.make_async_copy(kv_hbm, win.at[own_rows, :], own_sem)
    fetch_q = pltpu.make_async_copy(q_hbm, q, q_sem)
    fetch_kv.start()
    fetch_q.start()
    barrier = pltpu.get_barrier_semaphore()

    def greet(offset, carry):
        pl.semaphore_signal(
            barrier, inc=1, device_id={"req": lax.rem(me + offset, count)}, device_id_type=MESH
        )
        return carry

    lax.fori_loop(1, count, greet, 0)
    for slot in range(places):
        unused = [int(row[slot] is None) for row in lows]
        if any(unused):
            @pl.when(at_device(unused, me) == 1)
            def _():
                win[slot * CHUNK : (slot + 1) * CHUNK, :] = jnp.zeros((CHUNK, win.shape[1]), win.dtype)

    values[:, HD:] = jnp.ones((values.shape[0], HD), values.dtype)
    fetch_kv.wait()
    for first in range(0, info_ref.shape[0], TILE_Q):
        info_ref[first : first + TILE_Q, :] = jnp.transpose(facts_ref[:, first : first + TILE_Q])
    place_rows(stage, page_ref, 0, win.at[own_rows, :], facts_ref, 5)

    outgoing = []
    for r in range(rounds):
        row = []
        for j in range(max(len(s) for s in sends[r])):
            fields = [
                at_device([s[j][c] if len(s) > j else -1 for s in sends[r]], me) for c in range(4)
            ]
            row.append((j, *fields))
        outgoing.append(row)
    arriving = [
        [
            at_device([t[k] if len(t) > k else -1 for t in takes[r]], me)
            for k in range(max(len(t) for t in takes[r]))
        ]
        for r in range(rounds)
    ]

    def copy_of(r, j, k, g, target, source, slot):
        columns = pl.ds(pl.multiple_of(g * wide, wide), wide)
        return pltpu.make_async_remote_copy(
            src_ref=win.at[pl.ds(pl.multiple_of(source * CHUNK, CHUNK), CHUNK), columns],
            dst_ref=win.at[pl.ds(pl.multiple_of(slot * CHUNK, CHUNK), CHUNK), columns],
            send_sem=send_sem.at[r, j, g],
            recv_sem=recv_sem.at[r, k, g],
            device_id={"req": target},
            device_id_type=MESH,
        )

    def arrive(r, g):
        for k, slot in enumerate(arriving[r]):
            @pl.when(slot >= 0)
            def _():
                copy_of(r, 0, k, g, me, slot, slot).wait_recv()

    def launch(r, g):
        for j, target, source, slot, k in outgoing[r]:
            @pl.when(target >= 0)
            def _():
                copy_of(r, j, k, g, target, source, slot).start()

    def sent(r, g):
        for j, target, source, slot, k in outgoing[r]:
            @pl.when(target >= 0)
            def _():
                copy_of(r, j, k, g, me, source, slot).wait_send()

    def page_copy(offset):
        target = lax.rem(me + offset, count)
        return pltpu.make_async_remote_copy(
            src_ref=stage.at[pl.ds(pl.multiple_of(target * block, block), block), :],
            dst_ref=incoming.at[pl.ds(pl.multiple_of(offset * block, block), block), :],
            send_sem=page_send.at[offset],
            recv_sem=page_recv.at[offset],
            device_id={"req": target},
            device_id_type=MESH,
        )

    def tick(time):
        for r in range(rounds - 1, -1, -1):
            late = time - r
            g = lax.div(late, STAGGER)

            @pl.when((late >= 0) & (lax.rem(late, STAGGER) == 0) & (g < heads))
            def _():
                if r > 0:
                    arrive(r - 1, g)
                launch(r, g)

    pl.semaphore_wait(barrier, count - 1)
    tick(jnp.int32(0))
    low_here = [
        at_device([2 * count * 2 * CHUNK if row[slot] is None else row[slot] for row in lows], me)
        for slot in range(places + 2)
    ]
    for t in range(tiles):
        begin, stop, own, row = (info_ref[t * TILE_Q : (t + 1) * TILE_Q, c : c + 1] for c in range(4))
        for slot in range(places + 2):
            at = low_here[slot] + lax.broadcasted_iota(jnp.int32, (TILE_Q, CHUNK), 1)
            seen = (at <= row) & ((at >= own) | ((at >= begin) & (at < stop)))
            bias[t, :, slot * CHUNK : (slot + 1) * CHUNK] = jnp.where(seen, 0.0, NEG_FILL).astype(jnp.float32)
    lax.fori_loop(1, rounds, lambda time, carry: (tick(time), carry)[1], 0)

    def send_pages(offset, carry):
        page_copy(offset).start()
        return carry

    mine = pltpu.make_async_copy(
        stage.at[pl.ds(pl.multiple_of(me * block, block), block), :], incoming.at[0:block, :], self_sem
    )
    mine.start()
    fetch_q.wait()
    pair = 2 if per_group % 2 == 0 else 1
    parts = per_group // pair

    def tile(g, t, buffer, blocks):
        span = blocks * CHUNK
        rows = pl.ds(pl.multiple_of(t * TILE_Q, TILE_Q), TILE_Q)
        key_columns = pl.ds(pl.multiple_of(g * wide, wide), HD)
        live = jnp.concatenate([info_ref[rows, 3:4] >= info_ref[rows, 2:3]] * pair, axis=0)

        def score(part):
            stacked = jnp.concatenate(
                [
                    q[rows, pl.ds(pl.multiple_of(g * span_q + h * HD, HD), HD)]
                    for h in range(part * pair, (part + 1) * pair)
                ],
                axis=0,
            )
            raw = lax.dot_general(
                stacked, win[0:span, key_columns], (((1,), (1,)), ((), ())), preferred_element_type=jnp.float32
            )
            return (raw.reshape(pair, TILE_Q, span) + bias[t, :, 0:span][None]).reshape(pair * TILE_Q, span)

        ahead = score(0)
        for part in range(parts):
            now = ahead
            if part + 1 < parts:
                ahead = score(part + 1)
            top = jnp.max(now, axis=1, keepdims=True)
            weight = jnp.exp2((now - top) * FACTOR).astype(values.dtype)
            both = jnp.dot(weight, values[0:span, :], preferred_element_type=jnp.float32)
            total = jnp.where(live, both[:, HD:], 1.0)
            context = jnp.where(live, both[:, 0:HD] / total, 0.0).astype(done.dtype)
            for i in range(pair):
                h = part * pair + i
                done[buffer, :, h * HD : (h + 1) * HD] = context[i * TILE_Q : (i + 1) * TILE_Q, :]

    def out_copy(g, t, buffer):
        return pltpu.make_async_copy(
            done.at[buffer],
            out_hbm.at[
                pl.ds(pl.multiple_of(t * TILE_Q, TILE_Q), TILE_Q),
                pl.ds(pl.multiple_of(g * span_q, span_q), span_q),
            ],
            out_sem.at[buffer],
        )

    def step(index, carry):
        g, t, buffer = lax.div(index, tiles), lax.rem(index, tiles), lax.rem(index, 2)

        @pl.when(t == 0)
        def _():
            arrive(rounds - 1, g)
            values[:, 0:HD] = win[0 : values.shape[0], pl.ds(pl.multiple_of(g * wide + HD, HD), HD)]

        @pl.when(index >= 2)
        def _():
            out_copy(g, t, buffer).wait()

        @pl.when(t * TILE_Q < CHUNK)
        def _():
            tile(g, t, buffer, places + 1)

        @pl.when(t * TILE_Q >= CHUNK)
        def _():
            tile(g, t, buffer, places + 2)

        out_copy(g, t, buffer).start()
        tick(index + rounds)

        @pl.when(index == pages_at)
        def _():
            lax.fori_loop(1, count, send_pages, 0)

        return carry

    lax.fori_loop(0, steps, step, 0)
    for buffer in range(min(2, steps)):
        out_copy(0, 0, buffer).wait()

    def finish(g, carry):
        for r in range(rounds):
            sent(r, g)
        return carry

    lax.fori_loop(0, heads, finish, 0)

    def take_pages(offset, carry):
        page_copy(offset).wait()
        return carry

    lax.fori_loop(1, count, take_pages, 0)
    mine.wait()
    place_rows(cache_ref, facts_ref, 4, incoming, None, 0)


STAGGER = 3
PLACE_ROWS = 128


def answer_window(plan, queries, keys_values, facts, send_rows, per_group, capacity, collective_id):
    sends, takes, slots, lows = plan
    count = lax.axis_size("req")
    rows, cols = keys_values.shape
    heads = cols // (2 * HD)
    rounds = len(sends)
    outs = max(len(s) for r in sends for s in r)
    ins = max(len(t) for r in takes for t in r)
    span = len(lows[0]) * CHUNK
    vmem = pl.BlockSpec(memory_space=pltpu.VMEM)
    hbm = pl.BlockSpec(memory_space=pl.ANY)
    dma = pltpu.SemaphoreType.DMA
    flops = 4 * queries.size * span
    return pl.pallas_call(
        functools.partial(stream_kernel, plan, count, heads, per_group, capacity),
        out_shape=[
            jax.ShapeDtypeStruct(queries.shape, queries.dtype),
            jax.ShapeDtypeStruct((rows, cols), keys_values.dtype),
        ],
        in_specs=[vmem, vmem, hbm, hbm],
        out_specs=[hbm, vmem],
        scratch_shapes=[
            pltpu.VMEM((slots * CHUNK, cols), keys_values.dtype),
            pltpu.VMEM(queries.shape, queries.dtype),
            pltpu.VMEM((count * capacity * PAGE, cols), keys_values.dtype),
            pltpu.VMEM((count * capacity * PAGE, cols), keys_values.dtype),
            pltpu.VMEM((span, 2 * HD), keys_values.dtype),
            pltpu.VMEM((rows // TILE_Q, TILE_Q, span), jnp.float32),
            pltpu.VMEM((2, TILE_Q, per_group * HD), queries.dtype),
            pltpu.VMEM((rows, 8), jnp.int32),
            dma,
            dma,
            dma((rounds, outs, heads)),
            dma((rounds, ins, heads)),
            dma((count,)),
            dma((count,)),
            dma,
            dma((2,)),
        ],
        compiler_params=pltpu.CompilerParams(
            collective_id=collective_id, has_side_effects=True, vmem_limit_bytes=56 << 20
        ),
        cost_estimate=pl.CostEstimate(
            flops=flops, bytes_accessed=4 * (queries.size + keys_values.size), transcendentals=flops // (4 * HD)
        ),
        name="answer",
    )(send_rows, facts, queries, keys_values)


def block_table(lows, info, tiles, tile_q):
    blocks = lows.shape[0]
    low = lows[None, :]
    high = low + TILE_K
    begin, stop, own, row = (info[:, c : c + 1] for c in range(4))
    end = jnp.minimum(stop, row + 1)
    touched = ((low < end) & (high > begin)) | ((low <= row) & (high > own))
    whole = ((low >= begin) & (high <= end)) | ((low >= own) & (high <= row + 1))
    touched = jnp.any(touched.reshape(tiles, tile_q, blocks), axis=1)
    whole = jnp.all(whole.reshape(tiles, tile_q, blocks), axis=1)
    kind = jnp.where(touched, jnp.where(whole, 2, 1), 0).astype(jnp.int32)
    counts = jnp.sum(touched.astype(jnp.int32), axis=1)
    slots = jnp.arange(blocks, dtype=jnp.int32)
    before = touched[:, None, :] & (slots[None, None, :] < slots[None, :, None])
    place = jnp.sum(before.astype(jnp.int32), axis=2)
    pick = touched[:, None, :] & (place[:, None, :] == slots[None, :, None])
    table = jnp.sum(jnp.where(pick, slots[None, None, :], 0), axis=2)
    kinds = jnp.sum(jnp.where(pick, kind[:, None, :], 0), axis=2)
    return counts, table, kinds


def from_before(keys_values, group, offset):
    count = lax.axis_size("req")
    pairs = [
        (base + a, base + a + offset)
        for base in range(0, count, group)
        for a in range(group)
        if a + offset <= group and base + a + offset < count
    ]
    return lax.ppermute(keys_values, "req", pairs) if pairs else jnp.zeros_like(keys_values)


def full_window(keys_values, group, own_index):
    shard_rows = keys_values.shape[0]
    pieces = [from_before(keys_values, group, offset) for offset in range(group, 0, -1)]
    blocks = (group + 1) * shard_rows // TILE_K
    first = (own_index - group) * shard_rows
    return pieces + [keys_values], first + jnp.arange(blocks, dtype=jnp.int32) * TILE_K


def attend_kernel(
    pieces, tile_k, per_group, counts, blocks, kinds, lows, info_ref, q_ref, *refs
):
    kv_refs = refs[:pieces]
    refs = refs[pieces:]
    out_ref, kv, stacked, top, acc = refs
    tile = pl.program_id(1)
    tile_q = q_ref.shape[0]

    @pl.when(tile == 0)
    def _():
        at = 0
        for ref in kv_refs:
            kv[at : at + ref.shape[0], :] = ref[...]
            at += ref.shape[0]

    for head in range(per_group):
        stacked[pl.ds(head * tile_q, tile_q), :] = q_ref[:, head * HD : (head + 1) * HD]
    top[...] = jnp.full_like(top, NEG_FILL)
    acc[...] = jnp.zeros_like(acc)
    begin = info_ref[:, 0:1]
    stop = info_ref[:, 1:2]
    own = info_ref[:, 2:3]
    row = info_ref[:, 3:4]
    ones = jnp.ones((tile_k, HD), jnp.bfloat16)

    def block(slot, masked):
        start = pl.multiple_of(blocks[tile, slot] * tile_k, tile_k)
        key = kv[pl.ds(start, tile_k), 0:HD]
        value = jnp.concatenate([kv[pl.ds(start, tile_k), HD : 2 * HD], ones], axis=1)
        if masked:
            at = lows[blocks[tile, slot]] + lax.broadcasted_iota(jnp.int32, (tile_q, tile_k), 1)
            seen = (at <= row) & ((at >= own) | ((at >= begin) & (at < stop)))
            bias = jnp.where(seen, 0.0, NEG_FILL).astype(jnp.float32)
        chunk = min(CHUNK_HEADS, per_group)
        rows = chunk * tile_q
        for part in range(per_group // chunk):
            span = pl.ds(part * rows, rows)
            score = lax.dot_general(
                stacked[span, :], key, (((1,), (1,)), ((), ())),
                preferred_element_type=jnp.float32,
            )
            if masked:
                score = (score.reshape(chunk, tile_q, tile_k) + bias[None]).reshape(rows, tile_k)
            old = top[span, :]
            new = jnp.maximum(old, jnp.max(score, axis=1, keepdims=True))
            rescale = jnp.exp2((old - new) * FACTOR)
            weight = jnp.exp2((score - jnp.tile(new, (1, tile_k // HD))) * FACTOR)
            acc[span, :] = acc[span, :] * jnp.tile(rescale, (1, 2)) + jnp.dot(
                weight.astype(jnp.bfloat16), value, preferred_element_type=jnp.float32
            )
            top[span, :] = new

    def step(slot, carry):
        @pl.when(kinds[tile, slot] == 1)
        def _():
            block(slot, True)

        @pl.when(kinds[tile, slot] == 2)
        def _():
            block(slot, False)

        return carry

    lax.fori_loop(0, counts[tile], step, 0)
    live = row >= own
    for head in range(per_group):
        span = pl.ds(head * tile_q, tile_q)
        total = jnp.where(live, acc[span, HD : 2 * HD], 1.0)
        context = jnp.where(live, acc[span, 0:HD] / total, 0.0)
        out_ref[:, head * HD : (head + 1) * HD] = context.astype(out_ref.dtype)


def attend(queries, pieces, lows, info, key_heads, per_group):
    shard_rows = queries.shape[0]
    tile_q = min(TILE_Q, shard_rows)
    tile_k = TILE_K
    span_rows = sum(piece.shape[0] for piece in pieces)
    tiles = shard_rows // tile_q
    counts, table, kinds = block_table(lows, info, tiles, tile_q)
    wide = per_group * HD
    rows = per_group * tile_q
    flops = 4 * shard_rows * key_heads * wide * 1536
    return pl.pallas_call(
        functools.partial(attend_kernel, len(pieces), tile_k, per_group),
        out_shape=jax.ShapeDtypeStruct(queries.shape, jnp.bfloat16),
        grid_spec=pltpu.PrefetchScalarGridSpec(
            num_scalar_prefetch=4,
            grid=(key_heads, tiles),
            in_specs=[
                pl.BlockSpec((tile_q, info.shape[1]), lambda g, t, *_: (t, 0)),
                pl.BlockSpec((tile_q, wide), lambda g, t, *_: (t, g)),
            ]
            + [pl.BlockSpec((p.shape[0], 2 * HD), lambda g, t, *_: (0, g)) for p in pieces],
            out_specs=pl.BlockSpec((tile_q, wide), lambda g, t, *_: (t, g)),
            scratch_shapes=[
                pltpu.VMEM((span_rows, 2 * HD), jnp.bfloat16),
                pltpu.VMEM((rows, HD), jnp.bfloat16),
                pltpu.VMEM((rows, HD), jnp.float32),
                pltpu.VMEM((rows, 2 * HD), jnp.float32),
            ],
        ),
        compiler_params=pltpu.CompilerParams(vmem_limit_bytes=48 << 20),
        cost_estimate=pl.CostEstimate(
            flops=flops, bytes_accessed=4 * queries.size + 2 * span_rows * key_heads * 2 * HD,
            transcendentals=flops // (4 * HD),
        ),
        name="attend",
    )(counts, table, kinds, lows, info, queries, *pieces)


def pick_kernel(pages, index, source_ref, out_ref):
    def move(slot, carry):
        source = pl.multiple_of(index[slot] * PAGE, PAGE)
        target = pl.multiple_of(slot * PAGE, PAGE)
        out_ref[pl.ds(target, PAGE), :] = source_ref[pl.ds(source, PAGE), :]
        return carry

    lax.fori_loop(0, pages, move, 0)


def pick_pages(source, index):
    pages = index.shape[0]
    width = source.shape[1]
    return pl.pallas_call(
        functools.partial(pick_kernel, pages),
        out_shape=jax.ShapeDtypeStruct((pages * PAGE, width), source.dtype),
        grid_spec=pltpu.PrefetchScalarGridSpec(
            num_scalar_prefetch=1,
            grid=(1,),
            in_specs=[pl.BlockSpec(source.shape, lambda i, *_: (0, 0))],
            out_specs=pl.BlockSpec((pages * PAGE, width), lambda i, *_: (0, 0)),
        ),
        cost_estimate=pl.CostEstimate(
            flops=0, bytes_accessed=2 * (source.size + pages * PAGE * width), transcendentals=0
        ),
        name="pick",
    )(index, source)


def page_routes(cache_page, page_count, own_index, axis_size):
    capacity = (page_count + axis_size - 1) // axis_size
    all_pages = cache_page.shape[0]
    owners = cache_page // page_count
    by_source = owners.reshape(axis_size, page_count)
    page_iota = jnp.arange(page_count, dtype=jnp.int32)
    earlier = page_iota[None, :] < page_iota[:, None]
    same_owner = by_source[:, :, None] == by_source[:, None, :]
    rank = jnp.sum((same_owner & earlier[None]).astype(jnp.int32), axis=2)
    my_owner = lax.dynamic_index_in_dim(by_source, own_index, 0, keepdims=False)
    my_rank = lax.dynamic_index_in_dim(rank, own_index, 0, keepdims=False)
    target_slot = my_owner * capacity + my_rank
    slot_iota = jnp.arange(axis_size * capacity, dtype=jnp.int32)
    send_page = jnp.sum(
        jnp.where(slot_iota[:, None] == target_slot[None, :], page_iota[None, :], 0), axis=1
    )
    wanted = own_index * page_count + page_iota
    hits = cache_page[None, :] == wanted[:, None]
    source = jnp.arange(all_pages, dtype=jnp.int32) // page_count
    ranks = rank.reshape(-1)

    def arrival(place):
        return jnp.sum(jnp.where(hits, (place(source) * capacity + ranks)[None, :], 0), axis=1)

    return send_page, arrival, capacity


def rows_of(pages):
    return (pages[:, None] * PAGE + jnp.arange(PAGE, dtype=jnp.int32)[None, :]).reshape(-1)


def write_pages(keys_values, is_live, cache_page, own_index, axis_size, pieces):
    page_count = keys_values.shape[0] // PAGE
    send_page, arrival, _ = page_routes(cache_page, page_count, own_index, axis_size)
    masked = jnp.where(is_live[:, None], keys_values, jnp.zeros_like(keys_values))
    outgoing = pick_pages(masked, send_page)
    outgoing, pieces = lax.optimization_barrier((outgoing, pieces))
    incoming = lax.all_to_all(outgoing, "req", split_axis=0, concat_axis=0, tiled=True)
    return pick_pages(incoming, arrival(lambda source: source)), pieces


def on_device(queries, keys_values, seg_ids, cache_page):
    shard_rows = queries.shape[0]
    key_heads = keys_values.shape[1] // (2 * HD)
    per_group = queries.shape[1] // HD // key_heads
    tokens = seg_ids.shape[0]
    own_index = lax.axis_index("req")
    axis_size = lax.axis_size("req")
    group = STREAM // shard_rows

    ids = jnp.arange(tokens // STREAM * (REQS + 1), dtype=jnp.int32)
    position = jnp.arange(tokens, dtype=jnp.int32)
    member = seg_ids[None, :] == ids[:, None]
    starts = jnp.min(jnp.where(member, position[None, :], tokens), axis=1)
    stops = jnp.max(jnp.where(member, position[None, :], -1), axis=1) + 1

    query_rows = own_index * shard_rows + jnp.arange(shard_rows, dtype=jnp.int32)
    query_seg = lax.dynamic_slice_in_dim(seg_ids, own_index * shard_rows, shard_rows)
    is_live = query_seg >= 0
    shared = query_seg // (REQS + 1) * (REQS + 1)
    far = 2 * tokens
    is_shared = shared[:, None] == ids[None, :]
    is_own = query_seg[:, None] == ids[None, :]
    begin = jnp.sum(jnp.where(is_shared, starts[None, :], 0), axis=1)
    stop = jnp.sum(jnp.where(is_shared, stops[None, :], 0), axis=1)
    own = jnp.sum(jnp.where(is_own, starts[None, :], 0), axis=1)
    begin = jnp.where(is_live, begin, far)
    stop = jnp.where(is_live, stop, 0)
    own = jnp.where(is_live, own, far)
    zero = jnp.zeros_like(own)

    def whole_stream(q, kv):
        pieces, lows = full_window(kv, group, own_index)
        cache, pieces = write_pages(kv, is_live, cache_page, own_index, axis_size, pieces)
        info = jnp.stack([begin, stop, own, query_rows, zero, zero, zero, zero], axis=1)
        return attend(q, pieces, lows, info, key_heads, per_group), cache

    def windowed(rounds, near, collective_id, q, kv):
        plan = plan_of(rounds, axis_size, group, 2 * near)
        send_page, arrival, capacity = page_routes(cache_page, shard_rows // PAGE, own_index, axis_size)
        arrived = rows_of(arrival(lambda source: (own_index - source + axis_size) % axis_size))
        facts = jnp.stack([begin, stop, own, query_rows, arrived, is_live.astype(jnp.int32), zero, zero])
        return answer_window(
            plan, q, kv, facts, rows_of(send_page)[None, :], per_group, capacity, collective_id
        )

    prompt_ok = stops <= ids // (REQS + 1) * STREAM + LEAD + PROMPT_CHUNKS * CHUNK
    request_ok = (stops - 1) // shard_rows - starts // shard_rows <= NEAR
    short = jnp.all(jnp.where(ids % (REQS + 1) == 0, prompt_ok, request_ok))
    if group == 8 and shard_rows == 2 * CHUNK:
        context, cache = lax.cond(
            short, functools.partial(windowed, ROUNDS, NEAR, 0), whole_stream, queries, keys_values
        )
    else:
        context, cache = whole_stream(queries, keys_values)
    return (context, cache)


def solution(mesh):
    return jax.shard_map(
        on_device,
        mesh=mesh,
        in_specs=(P("req", "head"), P("req", "head"), P(), P()),
        out_specs=(P("req", "head"), P("req", "head")),
        check_vma=False,
    )
```

```python
import functools
import math

import jax
import jax.numpy as jnp
from jax import lax
from jax.experimental import pallas as pl
from jax.experimental.pallas import tpu as pltpu
from jax.sharding import PartitionSpec as P

HD = 128
STREAM = 4096
REQS = 6
PAGE = 16

NEG_FILL = -1e30
TILE_Q = 128
TILE_K = 256
CHUNK_HEADS = 4
CHUNK = 256
LEAD = 256
FACTOR = math.log2(math.e) / math.sqrt(HD)
MESH = pl.DeviceIdType.MESH

ROUNDS = (
    ((0, 1, 0), (0, 2, 0), (0, 4, 0), (1, 0, 2), (1, 3, 1), (1, 5, 1), (2, 3, 3), (2, 6, 4), (3, 1, 5), (3, 7, 6), (4, 5, 7), (4, 6, 7), (5, 7, 9), (6, 7, 11), (6, 10, 12), (7, 5, 13), (7, 11, 14)),
    ((0, 2, 2), (0, 4, 2), (1, 3, 2), (1, 5, 5), (2, 3, 4), (2, 6, 3), (3, 2, 1), (3, 7, 3), (4, 5, 8), (4, 6, 0), (4, 8, 0), (5, 4, 1), (5, 7, 10), (5, 9, 13), (6, 4, 4), (6, 7, 12), (6, 10, 11), (7, 5, 6), (7, 6, 9), (10, 8, 12), (11, 9, 14)),
    ((1, 5, 0), (2, 3, 0), (2, 6, 2), (3, 7, 2), (4, 5, 2), (4, 6, 8), (4, 8, 1), (5, 4, 5), (5, 7, 1), (6, 4, 3), (6, 7, 0), (6, 10, 3), (7, 5, 3), (7, 6, 10), (9, 8, 14), (10, 8, 11)),
    ((4, 8, 2), (5, 4, 6), (7, 6, 1), (9, 8, 13), (10, 8, 3)),
)
ROUNDS_LONG_REQUEST = (
    ((0, 1, 0), (0, 2, 0), (0, 4, 0), (1, 3, 2), (1, 5, 1), (2, 0, 4), (2, 3, 3), (2, 6, 3), (3, 2, 5), (3, 7, 6), (4, 5, 8), (4, 6, 7), (5, 7, 10), (5, 9, 9), (6, 7, 12), (6, 10, 11), (7, 5, 13), (7, 11, 14)),
    ((0, 4, 4), (1, 3, 1), (1, 5, 2), (2, 3, 4), (2, 6, 5), (3, 2, 2), (3, 7, 3), (4, 5, 7), (4, 6, 8), (4, 8, 0), (5, 4, 1), (5, 7, 9), (5, 9, 13), (6, 4, 3), (6, 7, 7), (6, 10, 12), (7, 5, 6), (7, 6, 10), (9, 8, 9), (10, 8, 11), (11, 9, 14)),
    ((1, 5, 0), (2, 3, 0), (2, 6, 2), (3, 2, 1), (3, 7, 2), (4, 5, 4), (4, 6, 1), (4, 8, 3), (5, 4, 2), (5, 7, 8), (5, 9, 2), (6, 4, 5), (6, 7, 11), (6, 10, 10), (7, 5, 3), (7, 6, 9), (9, 8, 13), (10, 8, 12)),
    ((3, 7, 1), (4, 5, 5), (4, 6, 0), (4, 8, 1), (5, 4, 6), (5, 7, 0), (7, 6, 6), (9, 8, 14), (10, 8, 10)),
    ((9, 8, 2),),
)
WINDOWS = ((ROUNDS, 4, 2), (ROUNDS_LONG_REQUEST, 4, 3))


def plan_of(rounds, count, group, prompt, near):
    places = prompt + near
    own = {i: {2 * i - 1: places, 2 * i: places + 1} for i in range(count)}
    held = [dict(own[i]) for i in range(count)]
    used = [[0, 0] for _ in range(count)]
    sends = [[[] for _ in range(count)] for _ in rounds]
    takes = [[[] for _ in range(count)] for _ in rounds]
    for index, transfers in enumerate(rounds):
        fresh = []
        for base in range(0, count, group):
            for source, target, chunk in transfers:
                u, v, c = base + source, base + target, 2 * base + chunk
                if u >= count or v >= count:
                    continue
                first = 2 * target - 1
                seen = target <= group and chunk < first and (chunk < prompt or chunk >= first - near)
                slot = used[v][0] if seen else places + 2 + used[v][1]
                used[v][0 if seen else 1] += 1
                fresh.append((v, c, slot))
                sends[index][u].append((v, held[u][c], slot, len(takes[index][v])))
                takes[index][v].append(slot)
        for v, c, slot in fresh:
            held[v][c] = slot
    slots = 1 + max(slot for h in held for slot in h.values())
    lows = [[None] * (places + 2) for _ in range(count)]
    for i, chunks in enumerate(held):
        for c, slot in chunks.items():
            if slot < places + 2:
                lows[i][slot] = LEAD + c * CHUNK
    return sends, takes, slots, lows


def at_device(values, me):
    common = max(set(values), key=values.count)
    result = common
    for i, value in enumerate(values):
        if value != common:
            result = jnp.where(me == i, value, result)
    return result


def column_of(ref, row, first, count):
    lanes = ref[row : row + 1, first : first + count]
    return jnp.transpose(jnp.broadcast_to(lanes, (8, count)))[:, 0:1]


def place_rows(out_ref, from_ref, from_row, source_ref, live_ref, live_row):
    height = source_ref.shape[0]
    at = lax.broadcasted_iota(jnp.int32, (PLACE_ROWS, height), 1)
    for first in range(0, out_ref.shape[0], PLACE_ROWS):
        chosen = column_of(from_ref, from_row, first, PLACE_ROWS) == at
        if live_ref is not None:
            chosen = chosen & (live_ref[live_row : live_row + 1, :] > 0)
        one_hot = jnp.where(chosen, 1.0, 0.0).astype(source_ref.dtype)
        out_ref[first : first + PLACE_ROWS, :] = jnp.dot(
            one_hot, source_ref[...], preferred_element_type=jnp.float32
        ).astype(out_ref.dtype)


def stream_kernel(plan, count, heads, per_group, capacity, page_ref, facts_ref, q_hbm, kv_hbm,
                  out_hbm, cache_ref, win, q, stage, incoming, values, bias, done, info_ref, own_sem, q_sem, send_sem, recv_sem,
                  page_send, page_recv, self_sem, out_sem):
    sends, takes, _, lows = plan
    me = lax.axis_index("req")
    rounds = len(sends)
    places = len(lows[0]) - 2
    own_rows = pl.ds(places * CHUNK, 2 * CHUNK)
    wide = 2 * HD
    span_q = per_group * HD
    tiles = q.shape[0] // TILE_Q
    steps = heads * tiles
    pages_at = min(steps - 1, STAGGER * (heads - 1) + 2)
    block = capacity * PAGE
    fetch_kv = pltpu.make_async_copy(kv_hbm, win.at[own_rows, :], own_sem)
    fetch_q = pltpu.make_async_copy(q_hbm, q, q_sem)
    fetch_kv.start()
    fetch_q.start()
    barrier = pltpu.get_barrier_semaphore()

    def greet(offset, carry):
        pl.semaphore_signal(
            barrier, inc=1, device_id={"req": lax.rem(me + offset, count)}, device_id_type=MESH
        )
        return carry

    lax.fori_loop(1, count, greet, 0)
    for slot in range(places):
        unused = [int(row[slot] is None) for row in lows]
        if any(unused):
            @pl.when(at_device(unused, me) == 1)
            def _():
                win[slot * CHUNK : (slot + 1) * CHUNK, :] = jnp.zeros((CHUNK, win.shape[1]), win.dtype)

    values[:, HD:] = jnp.ones((values.shape[0], HD), values.dtype)
    fetch_kv.wait()
    for first in range(0, info_ref.shape[0], TILE_Q):
        info_ref[first : first + TILE_Q, :] = jnp.transpose(facts_ref[:, first : first + TILE_Q])
    place_rows(stage, page_ref, 0, win.at[own_rows, :], facts_ref, 5)

    outgoing = []
    for r in range(rounds):
        row = []
        for j in range(max(len(s) for s in sends[r])):
            fields = [
                at_device([s[j][c] if len(s) > j else -1 for s in sends[r]], me) for c in range(4)
            ]
            row.append((j, *fields))
        outgoing.append(row)
    arriving = [
        [
            at_device([t[k] if len(t) > k else -1 for t in takes[r]], me)
            for k in range(max(len(t) for t in takes[r]))
        ]
        for r in range(rounds)
    ]

    def copy_of(r, j, k, g, target, source, slot):
        columns = pl.ds(pl.multiple_of(g * wide, wide), wide)
        return pltpu.make_async_remote_copy(
            src_ref=win.at[pl.ds(pl.multiple_of(source * CHUNK, CHUNK), CHUNK), columns],
            dst_ref=win.at[pl.ds(pl.multiple_of(slot * CHUNK, CHUNK), CHUNK), columns],
            send_sem=send_sem.at[r, j, g],
            recv_sem=recv_sem.at[r, k, g],
            device_id={"req": target},
            device_id_type=MESH,
        )

    def arrive(r, g):
        for k, slot in enumerate(arriving[r]):
            @pl.when(slot >= 0)
            def _():
                copy_of(r, 0, k, g, me, slot, slot).wait_recv()

    def launch(r, g):
        for j, target, source, slot, k in outgoing[r]:
            @pl.when(target >= 0)
            def _():
                copy_of(r, j, k, g, target, source, slot).start()

    def sent(r, g):
        for j, target, source, slot, k in outgoing[r]:
            @pl.when(target >= 0)
            def _():
                copy_of(r, j, k, g, me, source, slot).wait_send()

    def page_copy(offset):
        target = lax.rem(me + offset, count)
        return pltpu.make_async_remote_copy(
            src_ref=stage.at[pl.ds(pl.multiple_of(target * block, block), block), :],
            dst_ref=incoming.at[pl.ds(pl.multiple_of(offset * block, block), block), :],
            send_sem=page_send.at[offset],
            recv_sem=page_recv.at[offset],
            device_id={"req": target},
            device_id_type=MESH,
        )

    def tick(time):
        for r in range(rounds - 1, -1, -1):
            late = time - r
            g = lax.div(late, STAGGER)

            @pl.when((late >= 0) & (lax.rem(late, STAGGER) == 0) & (g < heads))
            def _():
                if r > 0:
                    arrive(r - 1, g)
                launch(r, g)

    pl.semaphore_wait(barrier, count - 1)
    tick(jnp.int32(0))
    low_here = [
        at_device([2 * count * 2 * CHUNK if row[slot] is None else row[slot] for row in lows], me)
        for slot in range(places + 2)
    ]
    for t in range(tiles):
        begin, stop, own, row = (info_ref[t * TILE_Q : (t + 1) * TILE_Q, c : c + 1] for c in range(4))
        for slot in range(places + 2):
            at = low_here[slot] + lax.broadcasted_iota(jnp.int32, (TILE_Q, CHUNK), 1)
            seen = (at <= row) & ((at >= own) | ((at >= begin) & (at < stop)))
            bias[t, :, slot * CHUNK : (slot + 1) * CHUNK] = jnp.where(seen, 0.0, NEG_FILL).astype(jnp.float32)
    lax.fori_loop(1, rounds, lambda time, carry: (tick(time), carry)[1], 0)

    def send_pages(offset, carry):
        page_copy(offset).start()
        return carry

    mine = pltpu.make_async_copy(
        stage.at[pl.ds(pl.multiple_of(me * block, block), block), :], incoming.at[0:block, :], self_sem
    )
    mine.start()
    fetch_q.wait()
    pair = 2 if per_group % 2 == 0 else 1
    parts = per_group // pair

    def tile(g, t, buffer, blocks):
        span = blocks * CHUNK
        rows = pl.ds(pl.multiple_of(t * TILE_Q, TILE_Q), TILE_Q)
        key_columns = pl.ds(pl.multiple_of(g * wide, wide), HD)
        live = jnp.concatenate([info_ref[rows, 3:4] >= info_ref[rows, 2:3]] * pair, axis=0)

        def score(part):
            stacked = jnp.concatenate(
                [
                    q[rows, pl.ds(pl.multiple_of(g * span_q + h * HD, HD), HD)]
                    for h in range(part * pair, (part + 1) * pair)
                ],
                axis=0,
            )
            raw = lax.dot_general(
                stacked, win[0:span, key_columns], (((1,), (1,)), ((), ())), preferred_element_type=jnp.float32
            )
            return (raw.reshape(pair, TILE_Q, span) + bias[t, :, 0:span][None]).reshape(pair * TILE_Q, span)

        ahead = score(0)
        for part in range(parts):
            now = ahead
            if part + 1 < parts:
                ahead = score(part + 1)
            top = jnp.max(now, axis=1, keepdims=True)
            weight = jnp.exp2((now - top) * FACTOR).astype(values.dtype)
            both = jnp.dot(weight, values[0:span, :], preferred_element_type=jnp.float32)
            total = jnp.where(live, both[:, HD:], 1.0)
            context = jnp.where(live, both[:, 0:HD] / total, 0.0).astype(done.dtype)
            for i in range(pair):
                h = part * pair + i
                done[buffer, :, h * HD : (h + 1) * HD] = context[i * TILE_Q : (i + 1) * TILE_Q, :]

    def out_copy(g, t, buffer):
        return pltpu.make_async_copy(
            done.at[buffer],
            out_hbm.at[
                pl.ds(pl.multiple_of(t * TILE_Q, TILE_Q), TILE_Q),
                pl.ds(pl.multiple_of(g * span_q, span_q), span_q),
            ],
            out_sem.at[buffer],
        )

    def step(index, carry):
        g, t, buffer = lax.div(index, tiles), lax.rem(index, tiles), lax.rem(index, 2)

        @pl.when(t == 0)
        def _():
            arrive(rounds - 1, g)
            values[:, 0:HD] = win[0 : values.shape[0], pl.ds(pl.multiple_of(g * wide + HD, HD), HD)]

        @pl.when(index >= 2)
        def _():
            out_copy(g, t, buffer).wait()

        @pl.when(t * TILE_Q < CHUNK)
        def _():
            tile(g, t, buffer, places + 1)

        @pl.when(t * TILE_Q >= CHUNK)
        def _():
            tile(g, t, buffer, places + 2)

        out_copy(g, t, buffer).start()
        tick(index + rounds)

        @pl.when(index == pages_at)
        def _():
            lax.fori_loop(1, count, send_pages, 0)

        return carry

    lax.fori_loop(0, steps, step, 0)
    for buffer in range(min(2, steps)):
        out_copy(0, 0, buffer).wait()

    def finish(g, carry):
        for r in range(rounds):
            sent(r, g)
        return carry

    lax.fori_loop(0, heads, finish, 0)

    def take_pages(offset, carry):
        page_copy(offset).wait()
        return carry

    lax.fori_loop(1, count, take_pages, 0)
    mine.wait()
    place_rows(cache_ref, facts_ref, 4, incoming, None, 0)


STAGGER = 3
PLACE_ROWS = 128


def answer_window(plan, queries, keys_values, facts, send_rows, per_group, capacity, collective_id):
    sends, takes, slots, lows = plan
    count = lax.axis_size("req")
    rows, cols = keys_values.shape
    heads = cols // (2 * HD)
    rounds = len(sends)
    outs = max(len(s) for r in sends for s in r)
    ins = max(len(t) for r in takes for t in r)
    span = len(lows[0]) * CHUNK
    vmem = pl.BlockSpec(memory_space=pltpu.VMEM)
    hbm = pl.BlockSpec(memory_space=pl.ANY)
    dma = pltpu.SemaphoreType.DMA
    flops = 4 * queries.size * span
    return pl.pallas_call(
        functools.partial(stream_kernel, plan, count, heads, per_group, capacity),
        out_shape=[
            jax.ShapeDtypeStruct(queries.shape, queries.dtype),
            jax.ShapeDtypeStruct((rows, cols), keys_values.dtype),
        ],
        in_specs=[vmem, vmem, hbm, hbm],
        out_specs=[hbm, vmem],
        scratch_shapes=[
            pltpu.VMEM((slots * CHUNK, cols), keys_values.dtype),
            pltpu.VMEM(queries.shape, queries.dtype),
            pltpu.VMEM((count * capacity * PAGE, cols), keys_values.dtype),
            pltpu.VMEM((count * capacity * PAGE, cols), keys_values.dtype),
            pltpu.VMEM((span, 2 * HD), keys_values.dtype),
            pltpu.VMEM((rows // TILE_Q, TILE_Q, span), jnp.float32),
            pltpu.VMEM((2, TILE_Q, per_group * HD), queries.dtype),
            pltpu.VMEM((rows, 8), jnp.int32),
            dma,
            dma,
            dma((rounds, outs, heads)),
            dma((rounds, ins, heads)),
            dma((count,)),
            dma((count,)),
            dma,
            dma((2,)),
        ],
        compiler_params=pltpu.CompilerParams(
            collective_id=collective_id, has_side_effects=True, vmem_limit_bytes=56 << 20
        ),
        cost_estimate=pl.CostEstimate(
            flops=flops, bytes_accessed=4 * (queries.size + keys_values.size), transcendentals=flops // (4 * HD)
        ),
        name="answer",
    )(send_rows, facts, queries, keys_values)


def block_table(lows, info, tiles, tile_q):
    blocks = lows.shape[0]
    low = lows[None, :]
    high = low + TILE_K
    begin, stop, own, row = (info[:, c : c + 1] for c in range(4))
    end = jnp.minimum(stop, row + 1)
    touched = ((low < end) & (high > begin)) | ((low <= row) & (high > own))
    whole = ((low >= begin) & (high <= end)) | ((low >= own) & (high <= row + 1))
    touched = jnp.any(touched.reshape(tiles, tile_q, blocks), axis=1)
    whole = jnp.all(whole.reshape(tiles, tile_q, blocks), axis=1)
    kind = jnp.where(touched, jnp.where(whole, 2, 1), 0).astype(jnp.int32)
    counts = jnp.sum(touched.astype(jnp.int32), axis=1)
    slots = jnp.arange(blocks, dtype=jnp.int32)
    before = touched[:, None, :] & (slots[None, None, :] < slots[None, :, None])
    place = jnp.sum(before.astype(jnp.int32), axis=2)
    pick = touched[:, None, :] & (place[:, None, :] == slots[None, :, None])
    table = jnp.sum(jnp.where(pick, slots[None, None, :], 0), axis=2)
    kinds = jnp.sum(jnp.where(pick, kind[:, None, :], 0), axis=2)
    return counts, table, kinds


def from_before(keys_values, group, offset):
    count = lax.axis_size("req")
    pairs = [
        (base + a, base + a + offset)
        for base in range(0, count, group)
        for a in range(group)
        if a + offset <= group and base + a + offset < count
    ]
    return lax.ppermute(keys_values, "req", pairs) if pairs else jnp.zeros_like(keys_values)


def full_window(keys_values, group, own_index):
    shard_rows = keys_values.shape[0]
    pieces = [from_before(keys_values, group, offset) for offset in range(group, 0, -1)]
    blocks = (group + 1) * shard_rows // TILE_K
    first = (own_index - group) * shard_rows
    return pieces + [keys_values], first + jnp.arange(blocks, dtype=jnp.int32) * TILE_K


def attend_kernel(
    pieces, tile_k, per_group, counts, blocks, kinds, lows, info_ref, q_ref, *refs
):
    kv_refs = refs[:pieces]
    refs = refs[pieces:]
    out_ref, kv, stacked, top, acc = refs
    tile = pl.program_id(1)
    tile_q = q_ref.shape[0]

    @pl.when(tile == 0)
    def _():
        at = 0
        for ref in kv_refs:
            kv[at : at + ref.shape[0], :] = ref[...]
            at += ref.shape[0]

    for head in range(per_group):
        stacked[pl.ds(head * tile_q, tile_q), :] = q_ref[:, head * HD : (head + 1) * HD]
    top[...] = jnp.full_like(top, NEG_FILL)
    acc[...] = jnp.zeros_like(acc)
    begin = info_ref[:, 0:1]
    stop = info_ref[:, 1:2]
    own = info_ref[:, 2:3]
    row = info_ref[:, 3:4]
    ones = jnp.ones((tile_k, HD), jnp.bfloat16)

    def block(slot, masked):
        start = pl.multiple_of(blocks[tile, slot] * tile_k, tile_k)
        key = kv[pl.ds(start, tile_k), 0:HD]
        value = jnp.concatenate([kv[pl.ds(start, tile_k), HD : 2 * HD], ones], axis=1)
        if masked:
            at = lows[blocks[tile, slot]] + lax.broadcasted_iota(jnp.int32, (tile_q, tile_k), 1)
            seen = (at <= row) & ((at >= own) | ((at >= begin) & (at < stop)))
            bias = jnp.where(seen, 0.0, NEG_FILL).astype(jnp.float32)
        chunk = min(CHUNK_HEADS, per_group)
        rows = chunk * tile_q
        for part in range(per_group // chunk):
            span = pl.ds(part * rows, rows)
            score = lax.dot_general(
                stacked[span, :], key, (((1,), (1,)), ((), ())),
                preferred_element_type=jnp.float32,
            )
            if masked:
                score = (score.reshape(chunk, tile_q, tile_k) + bias[None]).reshape(rows, tile_k)
            old = top[span, :]
            new = jnp.maximum(old, jnp.max(score, axis=1, keepdims=True))
            rescale = jnp.exp2((old - new) * FACTOR)
            weight = jnp.exp2((score - jnp.tile(new, (1, tile_k // HD))) * FACTOR)
            acc[span, :] = acc[span, :] * jnp.tile(rescale, (1, 2)) + jnp.dot(
                weight.astype(jnp.bfloat16), value, preferred_element_type=jnp.float32
            )
            top[span, :] = new

    def step(slot, carry):
        @pl.when(kinds[tile, slot] == 1)
        def _():
            block(slot, True)

        @pl.when(kinds[tile, slot] == 2)
        def _():
            block(slot, False)

        return carry

    lax.fori_loop(0, counts[tile], step, 0)
    live = row >= own
    for head in range(per_group):
        span = pl.ds(head * tile_q, tile_q)
        total = jnp.where(live, acc[span, HD : 2 * HD], 1.0)
        context = jnp.where(live, acc[span, 0:HD] / total, 0.0)
        out_ref[:, head * HD : (head + 1) * HD] = context.astype(out_ref.dtype)


def attend(queries, pieces, lows, info, key_heads, per_group):
    shard_rows = queries.shape[0]
    tile_q = min(TILE_Q, shard_rows)
    tile_k = TILE_K
    span_rows = sum(piece.shape[0] for piece in pieces)
    tiles = shard_rows // tile_q
    counts, table, kinds = block_table(lows, info, tiles, tile_q)
    wide = per_group * HD
    rows = per_group * tile_q
    flops = 4 * shard_rows * key_heads * wide * 1536
    return pl.pallas_call(
        functools.partial(attend_kernel, len(pieces), tile_k, per_group),
        out_shape=jax.ShapeDtypeStruct(queries.shape, jnp.bfloat16),
        grid_spec=pltpu.PrefetchScalarGridSpec(
            num_scalar_prefetch=4,
            grid=(key_heads, tiles),
            in_specs=[
                pl.BlockSpec((tile_q, info.shape[1]), lambda g, t, *_: (t, 0)),
                pl.BlockSpec((tile_q, wide), lambda g, t, *_: (t, g)),
            ]
            + [pl.BlockSpec((p.shape[0], 2 * HD), lambda g, t, *_: (0, g)) for p in pieces],
            out_specs=pl.BlockSpec((tile_q, wide), lambda g, t, *_: (t, g)),
            scratch_shapes=[
                pltpu.VMEM((span_rows, 2 * HD), jnp.bfloat16),
                pltpu.VMEM((rows, HD), jnp.bfloat16),
                pltpu.VMEM((rows, HD), jnp.float32),
                pltpu.VMEM((rows, 2 * HD), jnp.float32),
            ],
        ),
        compiler_params=pltpu.CompilerParams(vmem_limit_bytes=48 << 20),
        cost_estimate=pl.CostEstimate(
            flops=flops, bytes_accessed=4 * queries.size + 2 * span_rows * key_heads * 2 * HD,
            transcendentals=flops // (4 * HD),
        ),
        name="attend",
    )(counts, table, kinds, lows, info, queries, *pieces)


def pick_kernel(pages, index, source_ref, out_ref):
    def move(slot, carry):
        source = pl.multiple_of(index[slot] * PAGE, PAGE)
        target = pl.multiple_of(slot * PAGE, PAGE)
        out_ref[pl.ds(target, PAGE), :] = source_ref[pl.ds(source, PAGE), :]
        return carry

    lax.fori_loop(0, pages, move, 0)


def pick_pages(source, index):
    pages = index.shape[0]
    width = source.shape[1]
    return pl.pallas_call(
        functools.partial(pick_kernel, pages),
        out_shape=jax.ShapeDtypeStruct((pages * PAGE, width), source.dtype),
        grid_spec=pltpu.PrefetchScalarGridSpec(
            num_scalar_prefetch=1,
            grid=(1,),
            in_specs=[pl.BlockSpec(source.shape, lambda i, *_: (0, 0))],
            out_specs=pl.BlockSpec((pages * PAGE, width), lambda i, *_: (0, 0)),
        ),
        cost_estimate=pl.CostEstimate(
            flops=0, bytes_accessed=2 * (source.size + pages * PAGE * width), transcendentals=0
        ),
        name="pick",
    )(index, source)


def page_routes(cache_page, page_count, own_index, axis_size):
    capacity = (page_count + axis_size - 1) // axis_size
    all_pages = cache_page.shape[0]
    owners = cache_page // page_count
    by_source = owners.reshape(axis_size, page_count)
    page_iota = jnp.arange(page_count, dtype=jnp.int32)
    earlier = page_iota[None, :] < page_iota[:, None]
    same_owner = by_source[:, :, None] == by_source[:, None, :]
    rank = jnp.sum((same_owner & earlier[None]).astype(jnp.int32), axis=2)
    my_owner = lax.dynamic_index_in_dim(by_source, own_index, 0, keepdims=False)
    my_rank = lax.dynamic_index_in_dim(rank, own_index, 0, keepdims=False)
    target_slot = my_owner * capacity + my_rank
    slot_iota = jnp.arange(axis_size * capacity, dtype=jnp.int32)
    send_page = jnp.sum(
        jnp.where(slot_iota[:, None] == target_slot[None, :], page_iota[None, :], 0), axis=1
    )
    wanted = own_index * page_count + page_iota
    hits = cache_page[None, :] == wanted[:, None]
    source = jnp.arange(all_pages, dtype=jnp.int32) // page_count
    ranks = rank.reshape(-1)

    def arrival(place):
        return jnp.sum(jnp.where(hits, (place(source) * capacity + ranks)[None, :], 0), axis=1)

    return send_page, arrival, capacity


def rows_of(pages):
    return (pages[:, None] * PAGE + jnp.arange(PAGE, dtype=jnp.int32)[None, :]).reshape(-1)


def write_pages(keys_values, is_live, cache_page, own_index, axis_size, pieces):
    page_count = keys_values.shape[0] // PAGE
    send_page, arrival, _ = page_routes(cache_page, page_count, own_index, axis_size)
    masked = jnp.where(is_live[:, None], keys_values, jnp.zeros_like(keys_values))
    outgoing = pick_pages(masked, send_page)
    outgoing, pieces = lax.optimization_barrier((outgoing, pieces))
    incoming = lax.all_to_all(outgoing, "req", split_axis=0, concat_axis=0, tiled=True)
    return pick_pages(incoming, arrival(lambda source: source)), pieces


def on_device(queries, keys_values, seg_ids, cache_page):
    shard_rows = queries.shape[0]
    key_heads = keys_values.shape[1] // (2 * HD)
    per_group = queries.shape[1] // HD // key_heads
    tokens = seg_ids.shape[0]
    own_index = lax.axis_index("req")
    axis_size = lax.axis_size("req")
    group = STREAM // shard_rows

    ids = jnp.arange(tokens // STREAM * (REQS + 1), dtype=jnp.int32)
    position = jnp.arange(tokens, dtype=jnp.int32)
    member = seg_ids[None, :] == ids[:, None]
    starts = jnp.min(jnp.where(member, position[None, :], tokens), axis=1)
    stops = jnp.max(jnp.where(member, position[None, :], -1), axis=1) + 1

    query_rows = own_index * shard_rows + jnp.arange(shard_rows, dtype=jnp.int32)
    query_seg = lax.dynamic_slice_in_dim(seg_ids, own_index * shard_rows, shard_rows)
    is_live = query_seg >= 0
    shared = query_seg // (REQS + 1) * (REQS + 1)
    far = 2 * tokens
    is_shared = shared[:, None] == ids[None, :]
    is_own = query_seg[:, None] == ids[None, :]
    begin = jnp.sum(jnp.where(is_shared, starts[None, :], 0), axis=1)
    stop = jnp.sum(jnp.where(is_shared, stops[None, :], 0), axis=1)
    own = jnp.sum(jnp.where(is_own, starts[None, :], 0), axis=1)
    begin = jnp.where(is_live, begin, far)
    stop = jnp.where(is_live, stop, 0)
    own = jnp.where(is_live, own, far)
    zero = jnp.zeros_like(own)

    def whole_stream(q, kv):
        pieces, lows = full_window(kv, group, own_index)
        cache, pieces = write_pages(kv, is_live, cache_page, own_index, axis_size, pieces)
        info = jnp.stack([begin, stop, own, query_rows, zero, zero, zero, zero], axis=1)
        return attend(q, pieces, lows, info, key_heads, per_group), cache

    def windowed(collective_id, q, kv):
        rounds, prompt, near = WINDOWS[collective_id]
        plan = plan_of(rounds, axis_size, group, prompt, 2 * near)
        send_page, arrival, capacity = page_routes(cache_page, shard_rows // PAGE, own_index, axis_size)
        arrived = rows_of(arrival(lambda source: (own_index - source + axis_size) % axis_size))
        facts = jnp.stack([begin, stop, own, query_rows, arrived, is_live.astype(jnp.int32), zero, zero])
        return answer_window(
            plan, q, kv, facts, rows_of(send_page)[None, :], per_group, capacity, collective_id
        )

    is_prompt = ids % (REQS + 1) == 0
    prompt_rows = jnp.max(jnp.where(is_prompt, stops - ids // (REQS + 1) * STREAM - LEAD, 0))
    request_span = jnp.max(jnp.where(is_prompt, 0, (stops - 1) // shard_rows - starts // shard_rows))
    fits = [(prompt_rows <= prompt * CHUNK) & (request_span <= near) for _, prompt, near in WINDOWS]
    if group == 8 and shard_rows == 2 * CHUNK:
        run = whole_stream
        for index in range(len(WINDOWS) - 1, -1, -1):
            run = functools.partial(lax.cond, fits[index], functools.partial(windowed, index), run)
        context, cache = run(queries, keys_values)
    else:
        context, cache = whole_stream(queries, keys_values)
    return (context, cache)


def solution(mesh):
    return jax.shard_map(
        on_device,
        mesh=mesh,
        in_specs=(P("req", "head"), P("req", "head"), P(), P()),
        out_specs=(P("req", "head"), P("req", "head")),
        check_vma=False,
    )
```

```python
import functools
import math

import jax
import jax.numpy as jnp
from jax import lax
from jax.experimental import pallas as pl
from jax.experimental.pallas import tpu as pltpu
from jax.sharding import PartitionSpec as P

HD = 128
STREAM = 4096
REQS = 6
PAGE = 16

NEG_FILL = -1e30
TILE_Q = 128
TILE_K = 256
CHUNK_HEADS = 4
CHUNK = 256
LEAD = 256
FACTOR = math.log2(math.e) / math.sqrt(HD)
MESH = pl.DeviceIdType.MESH

ROUNDS = (
    ((0, 1, 0), (0, 2, 0), (0, 4, 0), (1, 0, 2), (1, 3, 1), (1, 5, 1), (2, 3, 3), (2, 6, 4), (3, 1, 5), (3, 7, 6), (4, 5, 7), (4, 6, 7), (5, 7, 9), (6, 7, 11), (6, 10, 12), (7, 5, 13), (7, 11, 14)),
    ((0, 2, 2), (0, 4, 2), (1, 3, 2), (1, 5, 5), (2, 3, 4), (2, 6, 3), (3, 2, 1), (3, 7, 3), (4, 5, 8), (4, 6, 0), (4, 8, 0), (5, 4, 1), (5, 7, 10), (5, 9, 13), (6, 4, 4), (6, 7, 12), (6, 10, 11), (7, 5, 6), (7, 6, 9), (10, 8, 12), (11, 9, 14)),
    ((1, 5, 0), (2, 3, 0), (2, 6, 2), (3, 7, 2), (4, 5, 2), (4, 6, 8), (4, 8, 1), (5, 4, 5), (5, 7, 1), (6, 4, 3), (6, 7, 0), (6, 10, 3), (7, 5, 3), (7, 6, 10), (9, 8, 14), (10, 8, 11)),
    ((4, 8, 2), (5, 4, 6), (7, 6, 1), (9, 8, 13), (10, 8, 3)),
)
ROUNDS_LONG_REQUEST = (
    ((0, 1, 0), (0, 2, 0), (0, 4, 0), (1, 3, 2), (1, 5, 1), (2, 0, 4), (2, 3, 3), (2, 6, 3), (3, 2, 5), (3, 7, 6), (4, 5, 8), (4, 6, 7), (5, 7, 10), (5, 9, 9), (6, 7, 12), (6, 10, 11), (7, 5, 13), (7, 11, 14)),
    ((0, 4, 4), (1, 3, 1), (1, 5, 2), (2, 3, 4), (2, 6, 5), (3, 2, 2), (3, 7, 3), (4, 5, 7), (4, 6, 8), (4, 8, 0), (5, 4, 1), (5, 7, 9), (5, 9, 13), (6, 4, 3), (6, 7, 7), (6, 10, 12), (7, 5, 6), (7, 6, 10), (9, 8, 9), (10, 8, 11), (11, 9, 14)),
    ((1, 5, 0), (2, 3, 0), (2, 6, 2), (3, 2, 1), (3, 7, 2), (4, 5, 4), (4, 6, 1), (4, 8, 3), (5, 4, 2), (5, 7, 8), (5, 9, 2), (6, 4, 5), (6, 7, 11), (6, 10, 10), (7, 5, 3), (7, 6, 9), (9, 8, 13), (10, 8, 12)),
    ((3, 7, 1), (4, 5, 5), (4, 6, 0), (4, 8, 1), (5, 4, 6), (5, 7, 0), (7, 6, 6), (9, 8, 14), (10, 8, 10)),
    ((9, 8, 2),),
)
WINDOWS = ((ROUNDS, 4, 2), (ROUNDS_LONG_REQUEST, 4, 3))


def plan_of(rounds, count, group, prompt, near):
    places = prompt + near
    own = {i: {2 * i - 1: places, 2 * i: places + 1} for i in range(count)}
    held = [dict(own[i]) for i in range(count)]
    used = [[0, 0] for _ in range(count)]
    sends = [[[] for _ in range(count)] for _ in rounds]
    takes = [[[] for _ in range(count)] for _ in rounds]
    for index, transfers in enumerate(rounds):
        fresh = []
        for base in range(0, count, group):
            for source, target, chunk in transfers:
                u, v, c = base + source, base + target, 2 * base + chunk
                if u >= count or v >= count:
                    continue
                first = 2 * target - 1
                seen = target <= group and chunk < first and (chunk < prompt or chunk >= first - near)
                slot = used[v][0] if seen else places + 2 + used[v][1]
                used[v][0 if seen else 1] += 1
                fresh.append((v, c, slot))
                sends[index][u].append((v, held[u][c], slot, len(takes[index][v])))
                takes[index][v].append(slot)
        for v, c, slot in fresh:
            held[v][c] = slot
    slots = 1 + max(slot for h in held for slot in h.values())
    lows = [[None] * (places + 2) for _ in range(count)]
    for i, chunks in enumerate(held):
        for c, slot in chunks.items():
            if slot < places + 2:
                lows[i][slot] = LEAD + c * CHUNK
    return sends, takes, slots, lows


def at_device(values, me):
    common = max(set(values), key=values.count)
    result = common
    for i, value in enumerate(values):
        if value != common:
            result = jnp.where(me == i, value, result)
    return result


def column_of(ref, row, first, count):
    lanes = ref[row : row + 1, first : first + count]
    return jnp.transpose(jnp.broadcast_to(lanes, (8, count)))[:, 0:1]


def place_rows(out_ref, from_ref, from_row, source_ref, live_ref, live_row):
    height = source_ref.shape[0]
    at = lax.broadcasted_iota(jnp.int32, (PLACE_ROWS, height), 1)
    for first in range(0, out_ref.shape[0], PLACE_ROWS):
        chosen = column_of(from_ref, from_row, first, PLACE_ROWS) == at
        if live_ref is not None:
            chosen = chosen & (live_ref[live_row : live_row + 1, :] > 0)
        one_hot = jnp.where(chosen, 1.0, 0.0).astype(source_ref.dtype)
        out_ref[first : first + PLACE_ROWS, :] = jnp.dot(
            one_hot, source_ref[...], preferred_element_type=jnp.float32
        ).astype(out_ref.dtype)


def stream_kernel(plan, count, heads, per_group, capacity, page_ref, facts_ref, q_hbm, kv_hbm,
                  out_hbm, cache_ref, win, q, stage, incoming, values, bias, done, info_ref, own_sem, q_sem, send_sem, recv_sem,
                  page_send, page_recv, self_sem, out_sem):
    sends, takes, _, lows = plan
    me = lax.axis_index("req")
    rounds = len(sends)
    places = len(lows[0]) - 2
    own_rows = pl.ds(places * CHUNK, 2 * CHUNK)
    wide = 2 * HD
    span_q = per_group * HD
    tiles = q.shape[0] // TILE_Q
    steps = heads * tiles
    pages_at = min(steps - 1, STAGGER * (heads - 1) + 2)
    block = capacity * PAGE
    fetch_kv = pltpu.make_async_copy(kv_hbm, win.at[own_rows, :], own_sem)
    fetch_q = pltpu.make_async_copy(q_hbm, q, q_sem)
    fetch_kv.start()
    fetch_q.start()
    barrier = pltpu.get_barrier_semaphore()

    def greet(offset, carry):
        pl.semaphore_signal(
            barrier, inc=1, device_id={"req": lax.rem(me + offset, count)}, device_id_type=MESH
        )
        return carry

    lax.fori_loop(1, count, greet, 0)
    fetch_kv.wait()
    outgoing = []
    for r in range(rounds):
        row = []
        for j in range(max(len(s) for s in sends[r])):
            fields = [
                at_device([s[j][c] if len(s) > j else -1 for s in sends[r]], me) for c in range(4)
            ]
            row.append((j, *fields))
        outgoing.append(row)
    arriving = [
        [
            at_device([t[k] if len(t) > k else -1 for t in takes[r]], me)
            for k in range(max(len(t) for t in takes[r]))
        ]
        for r in range(rounds)
    ]

    def copy_of(r, j, k, g, target, source, slot):
        columns = pl.ds(pl.multiple_of(g * wide, wide), wide)
        return pltpu.make_async_remote_copy(
            src_ref=win.at[pl.ds(pl.multiple_of(source * CHUNK, CHUNK), CHUNK), columns],
            dst_ref=win.at[pl.ds(pl.multiple_of(slot * CHUNK, CHUNK), CHUNK), columns],
            send_sem=send_sem.at[r, j, g],
            recv_sem=recv_sem.at[r, k, g],
            device_id={"req": target},
            device_id_type=MESH,
        )

    def arrive(r, g):
        for k, slot in enumerate(arriving[r]):
            @pl.when(slot >= 0)
            def _():
                copy_of(r, 0, k, g, me, slot, slot).wait_recv()

    def launch(r, g):
        for j, target, source, slot, k in outgoing[r]:
            @pl.when(target >= 0)
            def _():
                copy_of(r, j, k, g, target, source, slot).start()

    def sent(r, g):
        for j, target, source, slot, k in outgoing[r]:
            @pl.when(target >= 0)
            def _():
                copy_of(r, j, k, g, me, source, slot).wait_send()

    def page_copy(offset):
        target = lax.rem(me + offset, count)
        return pltpu.make_async_remote_copy(
            src_ref=stage.at[pl.ds(pl.multiple_of(target * block, block), block), :],
            dst_ref=incoming.at[pl.ds(pl.multiple_of(offset * block, block), block), :],
            send_sem=page_send.at[offset],
            recv_sem=page_recv.at[offset],
            device_id={"req": target},
            device_id_type=MESH,
        )

    def tick(time):
        for r in range(rounds - 1, -1, -1):
            late = time - r
            g = lax.div(late, STAGGER)

            @pl.when((late >= 0) & (lax.rem(late, STAGGER) == 0) & (g < heads))
            def _():
                if r > 0:
                    arrive(r - 1, g)
                launch(r, g)

    pl.semaphore_wait(barrier, count - 1)
    tick(jnp.int32(0))
    for slot in range(places):
        unused = [int(row[slot] is None) for row in lows]
        if any(unused):
            @pl.when(at_device(unused, me) == 1)
            def _():
                win[slot * CHUNK : (slot + 1) * CHUNK, :] = jnp.zeros((CHUNK, win.shape[1]), win.dtype)

    values[:, HD:] = jnp.ones((values.shape[0], HD), values.dtype)
    for first in range(0, info_ref.shape[0], TILE_Q):
        info_ref[first : first + TILE_Q, :] = jnp.transpose(facts_ref[:, first : first + TILE_Q])
    place_rows(stage, page_ref, 0, win.at[own_rows, :], facts_ref, 5)
    if rounds > 1:
        tick(jnp.int32(1))
    low_here = [
        at_device([2 * count * 2 * CHUNK if row[slot] is None else row[slot] for row in lows], me)
        for slot in range(places + 2)
    ]
    for t in range(tiles):
        begin, stop, own, row = (info_ref[t * TILE_Q : (t + 1) * TILE_Q, c : c + 1] for c in range(4))
        for slot in range(places + 2):
            at = low_here[slot] + lax.broadcasted_iota(jnp.int32, (TILE_Q, CHUNK), 1)
            seen = (at <= row) & ((at >= own) | ((at >= begin) & (at < stop)))
            bias[t, :, slot * CHUNK : (slot + 1) * CHUNK] = jnp.where(seen, 0.0, NEG_FILL).astype(jnp.float32)
    lax.fori_loop(min(2, rounds), rounds, lambda time, carry: (tick(time), carry)[1], 0)

    def send_pages(offset, carry):
        page_copy(offset).start()
        return carry

    mine = pltpu.make_async_copy(
        stage.at[pl.ds(pl.multiple_of(me * block, block), block), :], incoming.at[0:block, :], self_sem
    )
    mine.start()
    fetch_q.wait()
    pair = 2 if per_group % 2 == 0 else 1
    parts = per_group // pair

    def tile(g, t, buffer, blocks):
        span = blocks * CHUNK
        rows = pl.ds(pl.multiple_of(t * TILE_Q, TILE_Q), TILE_Q)
        key_columns = pl.ds(pl.multiple_of(g * wide, wide), HD)
        live = jnp.concatenate([info_ref[rows, 3:4] >= info_ref[rows, 2:3]] * pair, axis=0)

        def score(part):
            stacked = jnp.concatenate(
                [
                    q[rows, pl.ds(pl.multiple_of(g * span_q + h * HD, HD), HD)]
                    for h in range(part * pair, (part + 1) * pair)
                ],
                axis=0,
            )
            raw = lax.dot_general(
                stacked, win[0:span, key_columns], (((1,), (1,)), ((), ())), preferred_element_type=jnp.float32
            )
            return (raw.reshape(pair, TILE_Q, span) + bias[t, :, 0:span][None]).reshape(pair * TILE_Q, span)

        ahead = score(0)
        for part in range(parts):
            now = ahead
            if part + 1 < parts:
                ahead = score(part + 1)
            top = jnp.max(now, axis=1, keepdims=True)
            weight = jnp.exp2((now - top) * FACTOR).astype(values.dtype)
            both = jnp.dot(weight, values[0:span, :], preferred_element_type=jnp.float32)
            total = jnp.where(live, both[:, HD:], 1.0)
            context = jnp.where(live, both[:, 0:HD] / total, 0.0).astype(done.dtype)
            for i in range(pair):
                h = part * pair + i
                done[buffer, :, h * HD : (h + 1) * HD] = context[i * TILE_Q : (i + 1) * TILE_Q, :]

    def out_copy(g, t, buffer):
        return pltpu.make_async_copy(
            done.at[buffer],
            out_hbm.at[
                pl.ds(pl.multiple_of(t * TILE_Q, TILE_Q), TILE_Q),
                pl.ds(pl.multiple_of(g * span_q, span_q), span_q),
            ],
            out_sem.at[buffer],
        )

    def step(index, carry):
        g, t, buffer = lax.div(index, tiles), lax.rem(index, tiles), lax.rem(index, 2)

        @pl.when(t == 0)
        def _():
            arrive(rounds - 1, g)
            values[:, 0:HD] = win[0 : values.shape[0], pl.ds(pl.multiple_of(g * wide + HD, HD), HD)]

        @pl.when(index >= 2)
        def _():
            out_copy(g, t, buffer).wait()

        @pl.when(t * TILE_Q < CHUNK)
        def _():
            tile(g, t, buffer, places + 1)

        @pl.when(t * TILE_Q >= CHUNK)
        def _():
            tile(g, t, buffer, places + 2)

        out_copy(g, t, buffer).start()
        tick(index + rounds)

        @pl.when(index == pages_at)
        def _():
            lax.fori_loop(1, count, send_pages, 0)

        return carry

    lax.fori_loop(0, steps, step, 0)
    for buffer in range(min(2, steps)):
        out_copy(0, 0, buffer).wait()

    def finish(g, carry):
        for r in range(rounds):
            sent(r, g)
        return carry

    lax.fori_loop(0, heads, finish, 0)

    def take_pages(offset, carry):
        page_copy(offset).wait()
        return carry

    lax.fori_loop(1, count, take_pages, 0)
    mine.wait()
    place_rows(cache_ref, facts_ref, 4, incoming, None, 0)


STAGGER = 3
PLACE_ROWS = 128


def answer_window(plan, queries, keys_values, facts, send_rows, per_group, capacity, collective_id):
    sends, takes, slots, lows = plan
    count = lax.axis_size("req")
    rows, cols = keys_values.shape
    heads = cols // (2 * HD)
    rounds = len(sends)
    outs = max(len(s) for r in sends for s in r)
    ins = max(len(t) for r in takes for t in r)
    span = len(lows[0]) * CHUNK
    vmem = pl.BlockSpec(memory_space=pltpu.VMEM)
    hbm = pl.BlockSpec(memory_space=pl.ANY)
    dma = pltpu.SemaphoreType.DMA
    flops = 4 * queries.size * span
    return pl.pallas_call(
        functools.partial(stream_kernel, plan, count, heads, per_group, capacity),
        out_shape=[
            jax.ShapeDtypeStruct(queries.shape, queries.dtype),
            jax.ShapeDtypeStruct((rows, cols), keys_values.dtype),
        ],
        in_specs=[vmem, vmem, hbm, hbm],
        out_specs=[hbm, vmem],
        scratch_shapes=[
            pltpu.VMEM((slots * CHUNK, cols), keys_values.dtype),
            pltpu.VMEM(queries.shape, queries.dtype),
            pltpu.VMEM((count * capacity * PAGE, cols), keys_values.dtype),
            pltpu.VMEM((count * capacity * PAGE, cols), keys_values.dtype),
            pltpu.VMEM((span, 2 * HD), keys_values.dtype),
            pltpu.VMEM((rows // TILE_Q, TILE_Q, span), jnp.float32),
            pltpu.VMEM((2, TILE_Q, per_group * HD), queries.dtype),
            pltpu.VMEM((rows, 8), jnp.int32),
            dma,
            dma,
            dma((rounds, outs, heads)),
            dma((rounds, ins, heads)),
            dma((count,)),
            dma((count,)),
            dma,
            dma((2,)),
        ],
        compiler_params=pltpu.CompilerParams(
            collective_id=collective_id, has_side_effects=True, vmem_limit_bytes=56 << 20
        ),
        cost_estimate=pl.CostEstimate(
            flops=flops, bytes_accessed=4 * (queries.size + keys_values.size), transcendentals=flops // (4 * HD)
        ),
        name="answer",
    )(send_rows, facts, queries, keys_values)


def block_table(lows, info, tiles, tile_q):
    blocks = lows.shape[0]
    low = lows[None, :]
    high = low + TILE_K
    begin, stop, own, row = (info[:, c : c + 1] for c in range(4))
    end = jnp.minimum(stop, row + 1)
    touched = ((low < end) & (high > begin)) | ((low <= row) & (high > own))
    whole = ((low >= begin) & (high <= end)) | ((low >= own) & (high <= row + 1))
    touched = jnp.any(touched.reshape(tiles, tile_q, blocks), axis=1)
    whole = jnp.all(whole.reshape(tiles, tile_q, blocks), axis=1)
    kind = jnp.where(touched, jnp.where(whole, 2, 1), 0).astype(jnp.int32)
    counts = jnp.sum(touched.astype(jnp.int32), axis=1)
    slots = jnp.arange(blocks, dtype=jnp.int32)
    before = touched[:, None, :] & (slots[None, None, :] < slots[None, :, None])
    place = jnp.sum(before.astype(jnp.int32), axis=2)
    pick = touched[:, None, :] & (place[:, None, :] == slots[None, :, None])
    table = jnp.sum(jnp.where(pick, slots[None, None, :], 0), axis=2)
    kinds = jnp.sum(jnp.where(pick, kind[:, None, :], 0), axis=2)
    return counts, table, kinds


def from_before(keys_values, group, offset):
    count = lax.axis_size("req")
    pairs = [
        (base + a, base + a + offset)
        for base in range(0, count, group)
        for a in range(group)
        if a + offset <= group and base + a + offset < count
    ]
    return lax.ppermute(keys_values, "req", pairs) if pairs else jnp.zeros_like(keys_values)


def full_window(keys_values, group, own_index):
    shard_rows = keys_values.shape[0]
    pieces = [from_before(keys_values, group, offset) for offset in range(group, 0, -1)]
    blocks = (group + 1) * shard_rows // TILE_K
    first = (own_index - group) * shard_rows
    return pieces + [keys_values], first + jnp.arange(blocks, dtype=jnp.int32) * TILE_K


def attend_kernel(
    pieces, tile_k, per_group, counts, blocks, kinds, lows, info_ref, q_ref, *refs
):
    kv_refs = refs[:pieces]
    refs = refs[pieces:]
    out_ref, kv, stacked, top, acc = refs
    tile = pl.program_id(1)
    tile_q = q_ref.shape[0]

    @pl.when(tile == 0)
    def _():
        at = 0
        for ref in kv_refs:
            kv[at : at + ref.shape[0], :] = ref[...]
            at += ref.shape[0]

    for head in range(per_group):
        stacked[pl.ds(head * tile_q, tile_q), :] = q_ref[:, head * HD : (head + 1) * HD]
    top[...] = jnp.full_like(top, NEG_FILL)
    acc[...] = jnp.zeros_like(acc)
    begin = info_ref[:, 0:1]
    stop = info_ref[:, 1:2]
    own = info_ref[:, 2:3]
    row = info_ref[:, 3:4]
    ones = jnp.ones((tile_k, HD), jnp.bfloat16)

    def block(slot, masked):
        start = pl.multiple_of(blocks[tile, slot] * tile_k, tile_k)
        key = kv[pl.ds(start, tile_k), 0:HD]
        value = jnp.concatenate([kv[pl.ds(start, tile_k), HD : 2 * HD], ones], axis=1)
        if masked:
            at = lows[blocks[tile, slot]] + lax.broadcasted_iota(jnp.int32, (tile_q, tile_k), 1)
            seen = (at <= row) & ((at >= own) | ((at >= begin) & (at < stop)))
            bias = jnp.where(seen, 0.0, NEG_FILL).astype(jnp.float32)
        chunk = min(CHUNK_HEADS, per_group)
        rows = chunk * tile_q
        for part in range(per_group // chunk):
            span = pl.ds(part * rows, rows)
            score = lax.dot_general(
                stacked[span, :], key, (((1,), (1,)), ((), ())),
                preferred_element_type=jnp.float32,
            )
            if masked:
                score = (score.reshape(chunk, tile_q, tile_k) + bias[None]).reshape(rows, tile_k)
            old = top[span, :]
            new = jnp.maximum(old, jnp.max(score, axis=1, keepdims=True))
            rescale = jnp.exp2((old - new) * FACTOR)
            weight = jnp.exp2((score - jnp.tile(new, (1, tile_k // HD))) * FACTOR)
            acc[span, :] = acc[span, :] * jnp.tile(rescale, (1, 2)) + jnp.dot(
                weight.astype(jnp.bfloat16), value, preferred_element_type=jnp.float32
            )
            top[span, :] = new

    def step(slot, carry):
        @pl.when(kinds[tile, slot] == 1)
        def _():
            block(slot, True)

        @pl.when(kinds[tile, slot] == 2)
        def _():
            block(slot, False)

        return carry

    lax.fori_loop(0, counts[tile], step, 0)
    live = row >= own
    for head in range(per_group):
        span = pl.ds(head * tile_q, tile_q)
        total = jnp.where(live, acc[span, HD : 2 * HD], 1.0)
        context = jnp.where(live, acc[span, 0:HD] / total, 0.0)
        out_ref[:, head * HD : (head + 1) * HD] = context.astype(out_ref.dtype)


def attend(queries, pieces, lows, info, key_heads, per_group):
    shard_rows = queries.shape[0]
    tile_q = min(TILE_Q, shard_rows)
    tile_k = TILE_K
    span_rows = sum(piece.shape[0] for piece in pieces)
    tiles = shard_rows // tile_q
    counts, table, kinds = block_table(lows, info, tiles, tile_q)
    wide = per_group * HD
    rows = per_group * tile_q
    flops = 4 * shard_rows * key_heads * wide * 1536
    return pl.pallas_call(
        functools.partial(attend_kernel, len(pieces), tile_k, per_group),
        out_shape=jax.ShapeDtypeStruct(queries.shape, jnp.bfloat16),
        grid_spec=pltpu.PrefetchScalarGridSpec(
            num_scalar_prefetch=4,
            grid=(key_heads, tiles),
            in_specs=[
                pl.BlockSpec((tile_q, info.shape[1]), lambda g, t, *_: (t, 0)),
                pl.BlockSpec((tile_q, wide), lambda g, t, *_: (t, g)),
            ]
            + [pl.BlockSpec((p.shape[0], 2 * HD), lambda g, t, *_: (0, g)) for p in pieces],
            out_specs=pl.BlockSpec((tile_q, wide), lambda g, t, *_: (t, g)),
            scratch_shapes=[
                pltpu.VMEM((span_rows, 2 * HD), jnp.bfloat16),
                pltpu.VMEM((rows, HD), jnp.bfloat16),
                pltpu.VMEM((rows, HD), jnp.float32),
                pltpu.VMEM((rows, 2 * HD), jnp.float32),
            ],
        ),
        compiler_params=pltpu.CompilerParams(vmem_limit_bytes=48 << 20),
        cost_estimate=pl.CostEstimate(
            flops=flops, bytes_accessed=4 * queries.size + 2 * span_rows * key_heads * 2 * HD,
            transcendentals=flops // (4 * HD),
        ),
        name="attend",
    )(counts, table, kinds, lows, info, queries, *pieces)


def pick_kernel(pages, index, source_ref, out_ref):
    def move(slot, carry):
        source = pl.multiple_of(index[slot] * PAGE, PAGE)
        target = pl.multiple_of(slot * PAGE, PAGE)
        out_ref[pl.ds(target, PAGE), :] = source_ref[pl.ds(source, PAGE), :]
        return carry

    lax.fori_loop(0, pages, move, 0)


def pick_pages(source, index):
    pages = index.shape[0]
    width = source.shape[1]
    return pl.pallas_call(
        functools.partial(pick_kernel, pages),
        out_shape=jax.ShapeDtypeStruct((pages * PAGE, width), source.dtype),
        grid_spec=pltpu.PrefetchScalarGridSpec(
            num_scalar_prefetch=1,
            grid=(1,),
            in_specs=[pl.BlockSpec(source.shape, lambda i, *_: (0, 0))],
            out_specs=pl.BlockSpec((pages * PAGE, width), lambda i, *_: (0, 0)),
        ),
        cost_estimate=pl.CostEstimate(
            flops=0, bytes_accessed=2 * (source.size + pages * PAGE * width), transcendentals=0
        ),
        name="pick",
    )(index, source)


def page_routes(cache_page, page_count, own_index, axis_size):
    capacity = (page_count + axis_size - 1) // axis_size
    all_pages = cache_page.shape[0]
    owners = cache_page // page_count
    by_source = owners.reshape(axis_size, page_count)
    page_iota = jnp.arange(page_count, dtype=jnp.int32)
    earlier = page_iota[None, :] < page_iota[:, None]
    same_owner = by_source[:, :, None] == by_source[:, None, :]
    rank = jnp.sum((same_owner & earlier[None]).astype(jnp.int32), axis=2)
    my_owner = lax.dynamic_index_in_dim(by_source, own_index, 0, keepdims=False)
    my_rank = lax.dynamic_index_in_dim(rank, own_index, 0, keepdims=False)
    target_slot = my_owner * capacity + my_rank
    slot_iota = jnp.arange(axis_size * capacity, dtype=jnp.int32)
    send_page = jnp.sum(
        jnp.where(slot_iota[:, None] == target_slot[None, :], page_iota[None, :], 0), axis=1
    )
    wanted = own_index * page_count + page_iota
    hits = cache_page[None, :] == wanted[:, None]
    source = jnp.arange(all_pages, dtype=jnp.int32) // page_count
    ranks = rank.reshape(-1)

    def arrival(place):
        return jnp.sum(jnp.where(hits, (place(source) * capacity + ranks)[None, :], 0), axis=1)

    return send_page, arrival, capacity


def rows_of(pages):
    return (pages[:, None] * PAGE + jnp.arange(PAGE, dtype=jnp.int32)[None, :]).reshape(-1)


def write_pages(keys_values, is_live, cache_page, own_index, axis_size, pieces):
    page_count = keys_values.shape[0] // PAGE
    send_page, arrival, _ = page_routes(cache_page, page_count, own_index, axis_size)
    masked = jnp.where(is_live[:, None], keys_values, jnp.zeros_like(keys_values))
    outgoing = pick_pages(masked, send_page)
    outgoing, pieces = lax.optimization_barrier((outgoing, pieces))
    incoming = lax.all_to_all(outgoing, "req", split_axis=0, concat_axis=0, tiled=True)
    return pick_pages(incoming, arrival(lambda source: source)), pieces


def on_device(queries, keys_values, seg_ids, cache_page):
    shard_rows = queries.shape[0]
    key_heads = keys_values.shape[1] // (2 * HD)
    per_group = queries.shape[1] // HD // key_heads
    tokens = seg_ids.shape[0]
    own_index = lax.axis_index("req")
    axis_size = lax.axis_size("req")
    group = STREAM // shard_rows

    ids = jnp.arange(tokens // STREAM * (REQS + 1), dtype=jnp.int32)
    position = jnp.arange(tokens, dtype=jnp.int32)
    member = seg_ids[None, :] == ids[:, None]
    starts = jnp.min(jnp.where(member, position[None, :], tokens), axis=1)
    stops = jnp.max(jnp.where(member, position[None, :], -1), axis=1) + 1

    query_rows = own_index * shard_rows + jnp.arange(shard_rows, dtype=jnp.int32)
    query_seg = lax.dynamic_slice_in_dim(seg_ids, own_index * shard_rows, shard_rows)
    is_live = query_seg >= 0
    shared = query_seg // (REQS + 1) * (REQS + 1)
    far = 2 * tokens
    is_shared = shared[:, None] == ids[None, :]
    is_own = query_seg[:, None] == ids[None, :]
    begin = jnp.sum(jnp.where(is_shared, starts[None, :], 0), axis=1)
    stop = jnp.sum(jnp.where(is_shared, stops[None, :], 0), axis=1)
    own = jnp.sum(jnp.where(is_own, starts[None, :], 0), axis=1)
    begin = jnp.where(is_live, begin, far)
    stop = jnp.where(is_live, stop, 0)
    own = jnp.where(is_live, own, far)
    zero = jnp.zeros_like(own)

    def whole_stream(q, kv):
        pieces, lows = full_window(kv, group, own_index)
        cache, pieces = write_pages(kv, is_live, cache_page, own_index, axis_size, pieces)
        info = jnp.stack([begin, stop, own, query_rows, zero, zero, zero, zero], axis=1)
        return attend(q, pieces, lows, info, key_heads, per_group), cache

    def windowed(collective_id, q, kv):
        rounds, prompt, near = WINDOWS[collective_id]
        plan = plan_of(rounds, axis_size, group, prompt, 2 * near)
        send_page, arrival, capacity = page_routes(cache_page, shard_rows // PAGE, own_index, axis_size)
        arrived = rows_of(arrival(lambda source: (own_index - source + axis_size) % axis_size))
        facts = jnp.stack([begin, stop, own, query_rows, arrived, is_live.astype(jnp.int32), zero, zero])
        return answer_window(
            plan, q, kv, facts, rows_of(send_page)[None, :], per_group, capacity, collective_id
        )

    is_prompt = ids % (REQS + 1) == 0
    prompt_rows = jnp.max(jnp.where(is_prompt, stops - ids // (REQS + 1) * STREAM - LEAD, 0))
    request_span = jnp.max(jnp.where(is_prompt, 0, (stops - 1) // shard_rows - starts // shard_rows))
    fits = [(prompt_rows <= prompt * CHUNK) & (request_span <= near) for _, prompt, near in WINDOWS]
    if group == 8 and shard_rows == 2 * CHUNK:
        run = whole_stream
        for index in range(len(WINDOWS) - 1, -1, -1):
            run = functools.partial(lax.cond, fits[index], functools.partial(windowed, index), run)
        context, cache = run(queries, keys_values)
    else:
        context, cache = whole_stream(queries, keys_values)
    return (context, cache)


def solution(mesh):
    return jax.shard_map(
        on_device,
        mesh=mesh,
        in_specs=(P("req", "head"), P("req", "head"), P(), P()),
        out_specs=(P("req", "head"), P("req", "head")),
        check_vma=False,
    )
```
